32 devices in a mesh: rep: 8 (over z, y), grp: 4 (over x, core).
Axes of the slice: x: 2, y: 2, z: 4, core: 2. Of those that a mesh axis runs over, the one named last changes fastest.
Arguments:
- latents: bfloat16 [32768, 384], P(('rep', 'grp')), may hold values from -6 to 6
- condition: float32 [32, 384], P(('rep', 'grp')), may hold values from -6 to 6
- out_grad: bfloat16 [32768, 384], P(('rep', 'grp')), may hold values from -6 to 6
- master: float32 [20736, 128], P('grp')
- moment_one: float32 [20736, 128], P('grp'), may hold values from -512 to 512
- moment_two: float32 [20736, 128], P('grp'), may hold values from 1638 to 16384
- bias_master: float32 [5760], P('grp'), may hold values from -3 to 3
- bias_one: float32 [5760], P('grp'), may hold values from -512 to 512
- bias_two: float32 [5760], P('grp'), may hold values from 1638 to 16384
Outputs:
- block_out: bfloat16 [32768, 384], P(('rep', 'grp'))
- latent_grad: bfloat16 [32768, 384], P(('rep', 'grp'))
- condition_grad: float32 [32, 384], P(('rep', 'grp'))
- lamb_stats: float32 [3, 5], replicated
- new_master: float32 [20736, 128], P('grp')
- new_moment_one: float32 [20736, 128], P('grp')
- new_moment_two: float32 [20736, 128], P('grp')
- master_copy: bfloat16 [20736, 128], P('grp')
- new_bias: float32 [5760], P('grp')
- new_bias_one: float32 [5760], P('grp')
- new_bias_two: float32 [5760], P('grp')
- bias_copy: bfloat16 [5760], P('grp')
The draws below stay inside these ranges and needn't reach their ends.
All inputs are finite; a program needn't handle non-finite values.
Results may differ from the reference program's by a relative error of at most 0.0095.
The reference program's roundings to bfloat16 on the way count: a program that leaves them out, or rounds other values in their place, can miss the bound.
Values may be sent and summed in bfloat16 or wider, within the bound.
A program may use at most 128 MiB of HBM per device.

```python
import math
import jax
import jax.numpy as jnp
from jax import lax

D = 384
FF = 1536
HEADS = 6
HDIM = 64
LEN = 1024
SEQS = 32
TOKENS = 32768
SHARD_ROWS = 5184
BIAS_ALL = 5760
N_GRP = 4


def draw_master(key, part):
    extents = [D // N_GRP * 3 * D, D // N_GRP * D, D // N_GRP * FF, FF // N_GRP * D, D // N_GRP * 6 * D]
    spreads = [0.6 * D ** (-0.5), 4.0 * D ** (-0.5), D ** (-0.5), FF ** (-0.5), D ** (-0.5)]
    owner_width = sum(extents)
    factors = jnp.concatenate([jnp.full((extent,), spread, jnp.float32) for extent, spread in zip(extents, spreads)])
    positions = jnp.arange(N_GRP).astype(jnp.float32) / max(N_GRP - 1, 1)
    owner_scale = 3.0 ** (positions - 0.5)
    noise_draw = jnp.clip(jax.random.normal(key, (N_GRP, owner_width), jnp.float32), -4.0, 4.0)
    return (noise_draw * factors[None, :] * owner_scale[:, None]).reshape(N_GRP * SHARD_ROWS, 128)


def shard_levels(key, dims, cuts, smallest, largest):
    level = 1.0
    for axis_at, shards_of in cuts:
        draws = jax.random.uniform(jax.random.fold_in(jax.random.fold_in(key, 6), axis_at), (shards_of,), jnp.float32, smallest / len(cuts), largest / len(cuts))
        level = level * jnp.repeat(jnp.exp(draws), dims[axis_at] // shards_of).reshape((-1,) + (1,) * (len(dims) - 1 - axis_at))
    return level


def bell_draw(stream_key, dims, deviation, most, shards=(), held_as=jnp.bfloat16):
    factor_of = shard_levels(stream_key, dims, shards, -0.22, 0.18) if shards else 1.0
    entries = jax.random.normal(stream_key, dims, jnp.float32) * deviation * factor_of
    return jnp.minimum(jnp.maximum(entries, -most), most).astype(held_as)


def setup_inputs(seed: int = 0) -> dict:
    keys = jax.random.split(jax.random.key(seed), 10)
    return {
        "latents": bell_draw(keys[0], (TOKENS, D), 1.0, 6.0, ((0, 32),)),
        "condition": bell_draw(keys[1], (SEQS, D), 1.0, 6.0, ((0, 32),), jnp.float32),
        "out_grad": bell_draw(keys[2], (TOKENS, D), 1.0, 6.0, ((0, 32),)),
        "master": draw_master(jax.random.fold_in(keys[9], 71), 0),
        "moment_one": bell_draw(keys[4], (N_GRP * SHARD_ROWS, 128), (0.5 * TOKENS ** 0.5), 512.0, ((0, 4),), jnp.float32),
        "moment_two": jnp.clip(jnp.exp(math.log(16384.0) - 2.3028293 * jax.random.uniform(keys[5], (N_GRP * SHARD_ROWS, 128), jnp.float32) ** shard_levels(keys[5], (N_GRP * SHARD_ROWS, 128), ((0, 4),), -0.2, 0.2)), 1638.0, 16384.0),
        "bias_master": bell_draw(keys[6], (BIAS_ALL,), 0.2, 3.0, ((0, 4),), jnp.float32),
        "bias_one": bell_draw(keys[7], (BIAS_ALL,), (0.5 * TOKENS ** 0.5), 512.0, ((0, 4),), jnp.float32),
        "bias_two": jnp.clip(jnp.exp(math.log(16384.0) - 2.3028293 * jax.random.uniform(keys[8], (BIAS_ALL,), jnp.float32) ** shard_levels(keys[8], (BIAS_ALL,), ((0, 4),), -0.2, 0.2)), 1638.0, 16384.0),
    }


NORM_EPS = 1e-06
BETA_ONE = 0.5
BETA_TWO = 0.5
ADAM_EPS = 1e-06
STEP_RATE = 0.3
DECAY_RATE = 0.01
HIGH = lax.Precision.HIGHEST

@jax.custom_vjp
def low(v):
    return lax.optimization_barrier(v.astype(jnp.bfloat16)).astype(jnp.float32)

@jax.custom_vjp
def low_back(v):
    return v

def low_keep(v):
    return (low(v), None)

def low_pass(kept, grad):
    return (grad,)

def back_keep(v):
    return (v, None)

def back_low(kept, grad):
    return (low(grad),)
low.defvjp(low_keep, low_pass)
low_back.defvjp(back_keep, back_low)

def matrix_shapes():
    return [(D, 3 * D), (D, D), (D, FF), (FF, D), (D, 6 * D)]

def bias_lengths():
    return [3 * D, D, FF, D, 6 * D]

def owner_extents(groups):
    return [row_count // groups * col_count for row_count, col_count in matrix_shapes()]

def unpack(packed, bias_packed, groups):
    flattened = packed.reshape(groups, -1)
    matrices = []
    offset = 0
    for row_count, col_count in matrix_shapes():
        extent = row_count // groups * col_count
        matrices.append(flattened[:, offset:offset + extent].reshape(row_count, col_count))
        offset = offset + extent
    bias_rows = bias_packed.reshape(groups, -1)
    biases = []
    offset = 0
    for length in bias_lengths():
        extent = length // groups
        biases.append(bias_rows[:, offset:offset + extent].reshape(length))
        offset = offset + extent
    return (matrices, biases)

def pack(matrices, biases, groups):
    packed = jnp.concatenate([matrix.reshape(groups, -1) for matrix in matrices], axis=1).reshape(-1, 128)
    bias_packed = jnp.concatenate([vector.reshape(groups, -1) for vector in biases], axis=1).reshape(-1)
    return (packed, bias_packed)

def region_sums(values, groups):
    extents = owner_extents(groups)
    flattened = values.reshape(-1, sum(extents))
    totals = []
    offset = 0
    for extent in extents:
        totals.append(jnp.sum(flattened[:, offset:offset + extent]))
        offset = offset + extent
    return jnp.stack(totals)

def spread_ratio(ratio, groups):
    pieces = [jnp.broadcast_to(ratio[position], (extent,)) for position, extent in enumerate(owner_extents(groups))]
    return jnp.concatenate(pieces)

def lamb_step(master, moment_one, moment_two, grads, groups, combine):
    new_one = BETA_ONE * moment_one + (1.0 - BETA_ONE) * grads
    new_two = BETA_TWO * moment_two + (1.0 - BETA_TWO) * grads * grads
    update = new_one / (jnp.sqrt(new_two) + ADAM_EPS) + DECAY_RATE * master
    weight_sq, update_sq = combine(region_sums(master * master, groups), region_sums(update * update, groups))
    weight_norm = jnp.sqrt(weight_sq)
    update_norm = jnp.sqrt(update_sq)
    ratio = weight_norm / (update_norm + NORM_EPS)
    owner_width = sum(owner_extents(groups))
    scaled = (update.reshape(-1, owner_width) * spread_ratio(ratio, groups)[None, :]).reshape(update.shape)
    new_master = master - STEP_RATE * scaled
    return (new_master, new_one, new_two, jnp.stack([weight_norm, update_norm, ratio]))

def adam_step(values, moment_one, moment_two, grads):
    new_one = BETA_ONE * moment_one + (1.0 - BETA_ONE) * grads
    new_two = BETA_TWO * moment_two + (1.0 - BETA_TWO) * grads * grads
    return (values - STEP_RATE * new_one / (jnp.sqrt(new_two) + ADAM_EPS), new_one, new_two)

def keep_both(weight_part, update_part):
    return (weight_part, update_part)

def modulated_norm(values, shift, scaling):
    centered = values - lax.optimization_barrier(jnp.mean(values, axis=-1, keepdims=True))
    variance = lax.optimization_barrier(jnp.mean(centered * centered, axis=-1, keepdims=True))
    normed = centered * lax.rsqrt(variance + NORM_EPS)
    return normed * (1.0 + scaling[:, None, :]) + shift[:, None, :]

def gelu_tanh(values):
    return jax.nn.gelu(values, approximate=True)

def project(values, matrix):
    return jnp.einsum('...i,ij->...j', values, matrix, precision=HIGH)

def attention(queries, key_rows, value_rows):
    groups, length = (queries.shape[0], queries.shape[1])
    block_rows = min(512, length)
    score_scale = HDIM ** (-0.5)

    def one_block(query_block):
        scores = low_back(jnp.einsum('gqhe,gkhe->ghqk', query_block, key_rows, precision=HIGH) * score_scale)
        weights_soft = jax.nn.softmax(scores, axis=-1)
        return jnp.einsum('ghqk,gkhe->gqhe', low(weights_soft), value_rows, precision=HIGH)
    blocks = jnp.moveaxis(queries.reshape(groups, length // block_rows, block_rows, HEADS, HDIM), 1, 0)
    attended = lax.map(jax.checkpoint(one_block), blocks)
    return jnp.moveaxis(attended, 0, 1).reshape(groups, length, HEADS * HDIM)

def block_forward(params, latents, condition):
    matrices, biases = params
    w_qkv, w_out, up_weight, down_weight, w_ada = matrices
    b_qkv, b_out, b_up, down_projection_bias, b_ada = biases
    groups, length = (latents.shape[0], latents.shape[1])
    cond_act = low(jax.nn.silu(condition))
    modulation = low_back(project(cond_act, w_ada) + b_ada)
    shift_one, scale_one, gate_one, shift_two, scale_two, gate_two = jnp.split(modulation, 6, axis=-1)
    normed_one = low(modulated_norm(latents, shift_one, scale_one))
    projected = low(low_back(project(normed_one, w_qkv) + b_qkv))
    heads_view = projected.reshape(groups, length, 3, HEADS, HDIM)
    attended = attention(heads_view[:, :, 0], heads_view[:, :, 1], heads_view[:, :, 2])
    attended = low(low_back(attended))
    branch_one = low_back(project(attended, w_out) + b_out)
    middle = latents + gate_one[:, None, :] * branch_one
    normed_two = low(modulated_norm(middle, shift_two, scale_two))
    hidden_pre = low_back(project(normed_two, up_weight) + b_up)
    hidden = low(gelu_tanh(hidden_pre))
    branch_two = low_back(project(hidden, down_weight) + down_projection_bias)
    return middle + gate_two[:, None, :] * branch_two

def reference(latents, condition, out_grad, master, moment_one, moment_two, bias_master, bias_one, bias_two):
    matrices, biases = unpack(master, bias_master, N_GRP)
    params = ([low(matrix) for matrix in matrices], [low(vector) for vector in biases])
    group_size = math.gcd(SEQS, max(1, 4096 // LEN))
    group_count = SEQS // group_size
    latent_groups = latents.astype(jnp.float32).reshape(group_count, group_size, LEN, D)
    condition_groups = condition.reshape(group_count, group_size, D)
    cotangent_groups = out_grad.astype(jnp.float32).reshape(group_count, group_size, LEN, D)
    zeros_init = jax.tree.map(jnp.zeros_like, params)

    def one_group(totals, items):
        group_latents, group_condition, group_cotangent = items
        outputs, pullback = jax.vjp(block_forward, params, group_latents, group_condition)
        grad_params, grad_latents, grad_condition = pullback(group_cotangent)
        totals = jax.tree.map(jnp.add, totals, grad_params)
        return (totals, (outputs.astype(jnp.bfloat16), grad_latents.astype(jnp.bfloat16), grad_condition))
    grad_totals, stacked = lax.scan(one_group, zeros_init, (latent_groups, condition_groups, cotangent_groups))
    outputs, latent_grads, condition_grads = stacked
    grad_pack, bias_pack = pack(grad_totals[0], grad_totals[1], N_GRP)
    new_master, new_one, new_two, lamb_stats = lamb_step(master, moment_one, moment_two, grad_pack, N_GRP, keep_both)
    new_bias, new_bias_one, new_bias_two = adam_step(bias_master, bias_one, bias_two, bias_pack)
    return (outputs.reshape(TOKENS, D), latent_grads.reshape(TOKENS, D), condition_grads.reshape(SEQS, D), lamb_stats, new_master, new_one, new_two, new_master.astype(jnp.bfloat16), new_bias, new_bias_one, new_bias_two, new_bias.astype(jnp.bfloat16))
```

```python
import functools

import jax
import jax.numpy as jnp
from jax import lax
from jax.experimental import pallas as pl
from jax.experimental.pallas import tpu as pltpu
from jax.sharding import PartitionSpec as P

D = 384
FF = 1536
HEADS = 6
HDIM = 64
PAIRS = HEADS // 2

NORM_EPS = 1e-06
BETA_ONE = 0.5
BETA_TWO = 0.5
ADAM_EPS = 1e-06
STEP_RATE = 0.3
DECAY_RATE = 0.01

F32 = jnp.float32
BF16 = jnp.bfloat16
NN = ((1,), (0,))
NT = ((1,), (1,))
TN = ((0,), (0,))
GELU_A = 0.044715
GELU_C = 0.7978845608028654


def dot(a, b, dims=NN):
    return lax.dot_general(a, b, (dims, ((), ())), preferred_element_type=F32)


def matrix_shapes():
    return [(D, 3 * D), (D, D), (D, FF), (FF, D), (D, 6 * D)]


def bias_lengths():
    return [3 * D, D, FF, D, 6 * D]


def owner_extents(groups):
    return [row_count // groups * col_count for row_count, col_count in matrix_shapes()]


def unpack(packed, bias_packed, groups):
    flattened = packed.reshape(groups, -1)
    matrices = []
    offset = 0
    for row_count, col_count in matrix_shapes():
        extent = row_count // groups * col_count
        matrices.append(flattened[:, offset : offset + extent].reshape(row_count, col_count))
        offset = offset + extent
    bias_rows = bias_packed.reshape(groups, -1)
    biases = []
    offset = 0
    for length in bias_lengths():
        extent = length // groups
        biases.append(bias_rows[:, offset : offset + extent].reshape(length))
        offset = offset + extent
    return (matrices, biases)


def pack(matrices, biases, groups):
    packed = jnp.concatenate([matrix.reshape(groups, -1) for matrix in matrices], axis=1).reshape(
        -1, 128
    )
    bias_packed = jnp.concatenate(
        [vector.reshape(groups, -1) for vector in biases], axis=1
    ).reshape(-1)
    return (packed, bias_packed)


def region_sums(values, groups):
    extents = owner_extents(groups)
    flattened = values.reshape(-1, sum(extents))
    totals = []
    offset = 0
    for extent in extents:
        totals.append(jnp.sum(flattened[:, offset : offset + extent]))
        offset = offset + extent
    return jnp.stack(totals)


def spread_ratio(ratio, groups):
    pieces = [
        jnp.broadcast_to(ratio[position], (extent,))
        for position, extent in enumerate(owner_extents(groups))
    ]
    return jnp.concatenate(pieces)


def lamb_step(master, moment_one, moment_two, grads, groups, combine):
    new_one = BETA_ONE * moment_one + (1.0 - BETA_ONE) * grads
    new_two = BETA_TWO * moment_two + (1.0 - BETA_TWO) * grads * grads
    update = new_one / (jnp.sqrt(new_two) + ADAM_EPS) + DECAY_RATE * master
    weight_sq, update_sq = combine(
        region_sums(master * master, groups), region_sums(update * update, groups)
    )
    weight_norm = jnp.sqrt(weight_sq)
    update_norm = jnp.sqrt(update_sq)
    ratio = weight_norm / (update_norm + NORM_EPS)
    owner_width = sum(owner_extents(groups))
    scaled = (update.reshape(-1, owner_width) * spread_ratio(ratio, groups)[None, :]).reshape(
        update.shape
    )
    new_master = master - STEP_RATE * scaled
    return (new_master, new_one, new_two, jnp.stack([weight_norm, update_norm, ratio]))


def adam_step(values, moment_one, moment_two, grads):
    new_one = BETA_ONE * moment_one + (1.0 - BETA_ONE) * grads
    new_two = BETA_TWO * moment_two + (1.0 - BETA_TWO) * grads * grads
    return (values - STEP_RATE * new_one / (jnp.sqrt(new_two) + ADAM_EPS), new_one, new_two)


def norm_totals(weight_part, update_part):
    return lax.psum((weight_part, update_part), "grp")


def mean_last(v):
    return jnp.sum(v, axis=-1, keepdims=True) * (1.0 / v.shape[-1])


def normalise(v):
    centered = v - mean_last(v)
    r = lax.rsqrt(mean_last(centered * centered) + NORM_EPS)
    return centered * r, r


def norm_back(e, n, r):
    return r * (e - mean_last(e) - n * mean_last(e * n))


def fold(v):
    return jnp.sum(v.reshape(v.shape[0] // 8, 8, v.shape[1]), axis=0)


def lanes_of(j, rows):
    lane = lax.broadcasted_iota(jnp.int32, (rows, 2 * HDIM), 1)
    return (lane >= HDIM) if j else (lane < HDIM)


def block_kernel(
    lat, og, mod, w_qkv, w_out, w_up, w_down, b_qkv, b_out, b_up, b_down,
    out_o, latg_o, gqkv_o, gout_o, gup_o, gdown_o, bqkv_o, bout_o, bup_o, bdown_o, dmod_o,
    nm1, q3, k3, v3, att, lse, datt, dpj, dqs, nm2, hid, dhid, db2, db1, dmid, acc,
):
    length = lat.shape[0]
    tile = 256
    tiles = length // tile
    shift1, scale1, gate1 = mod[0:1, :], mod[1:2, :] + 1.0, mod[2:3, :]
    shift2, scale2, gate2 = mod[3:4, :], mod[4:5, :] + 1.0, mod[5:6, :]

    def qkv_tile(t, _):
        rows = pl.ds(pl.multiple_of(t * tile, tile), tile)
        n, _r = normalise(lat[rows, :].astype(F32))
        normed = (n * scale1 + shift1).astype(BF16)
        nm1[rows, :] = normed
        proj = (dot(normed, w_qkv[...]) + b_qkv[...]).astype(BF16)
        for p in range(PAIRS):
            q3[p, rows, :] = proj[:, 128 * p : 128 * p + 128] * jnp.asarray(HDIM**-0.5, BF16)
            k3[p, rows, :] = proj[:, D + 128 * p : D + 128 * p + 128]
            v3[p, rows, :] = proj[:, 2 * D + 128 * p : 2 * D + 128 * p + 128]
        return 0

    lax.fori_loop(0, tiles, qkv_tile, 0)

    qb = 256

    def att_pair(i, _):
        p = i // (length // qb)
        rows = pl.ds(pl.multiple_of((i % (length // qb)) * qb, qb), qb)
        q = q3[p, rows, :]
        outs, stats = [], []
        for j in range(2):
            qj = jnp.where(lanes_of(j, qb), q, jnp.zeros_like(q))
            s = dot(qj, k3[p], NT)
            m = jnp.max(s, axis=-1, keepdims=True)
            e = jnp.exp(s - m)
            l = jnp.sum(e, axis=-1, keepdims=True)
            outs.append(dot((e * (1.0 / l)).astype(BF16), v3[p]))
            stats.append(m + jnp.log(l))
        att[p, rows, :] = jnp.where(lanes_of(0, qb), outs[0], outs[1]).astype(BF16)
        lane = lax.broadcasted_iota(jnp.int32, (qb, 128), 1)
        lse[p, rows, :] = jnp.where(lane == 0, stats[0], stats[1])
        return 0

    lax.fori_loop(0, PAIRS * (length // qb), att_pair, 0)

    acc[...] = jnp.zeros_like(acc)

    def mlp_tile(t, _):
        rows = pl.ds(pl.multiple_of(t * tile, tile), tile)
        at = jnp.concatenate([att[p, rows, :] for p in range(PAIRS)], axis=1)
        branch1 = dot(at, w_out[...]) + b_out[...]
        mid = lat[rows, :].astype(F32) + gate1 * branch1
        n2, r2 = normalise(mid)
        normed = (n2 * scale2 + shift2).astype(BF16)
        nm2[rows, :] = normed
        pre = dot(normed, w_up[...]) + b_up[...]
        sq = pre * pre
        th = jnp.tanh(pre * (GELU_C + (GELU_C * GELU_A) * sq))
        half = 0.5 + 0.5 * th
        h = (pre * half).astype(BF16)
        hid[rows, :] = h
        slope = half + (0.5 * pre) * (1.0 - th * th) * (GELU_C + (3.0 * GELU_C * GELU_A) * sq)
        branch2 = dot(h, w_down[...]) + b_down[...]
        g = og[rows, :].astype(F32)
        out_o[rows, :] = (mid + gate2 * branch2).astype(BF16)
        d2 = (gate2 * g).astype(BF16)
        db2[rows, :] = d2
        dh = (dot(d2, w_down[...], NT) * slope).astype(BF16)
        dhid[rows, :] = dh
        dn2 = dot(dh, w_up[...], NT)
        dm = g + norm_back(dn2 * scale2, n2, r2)
        dmid[rows, :] = dm
        d1 = (gate1 * dm).astype(BF16)
        db1[rows, :] = d1
        da = dot(d1, w_out[...], NT).astype(BF16)
        for p in range(PAIRS):
            datt[p, rows, :] = da[:, 128 * p : 128 * p + 128]
        acc[2, :, 0:D] += fold(dm * branch1)
        acc[3, :, 0:D] += fold(dn2)
        acc[4, :, 0:D] += fold(dn2 * n2)
        acc[5, :, 0:D] += fold(g * branch2)
        acc[6, :, 0:D] += fold(d1.astype(F32))
        acc[7, :, 0:D] += fold(d2.astype(F32))
        acc[8, :, :] += fold(dh.astype(F32))
        return 0

    lax.fori_loop(0, tiles, mlp_tile, 0)

    def gmlp(c, _):
        cols = pl.ds(pl.multiple_of(c * D, D), D)
        gdown_o[cols, :] = dot(hid[:, cols], db2[...], TN)
        gup_o[:, cols] = dot(nm2[...], dhid[:, cols], TN)
        return 0

    lax.fori_loop(0, FF // D, gmlp, 0)
    for p in range(PAIRS):
        gout_o[128 * p : 128 * p + 128, :] = dot(att[p], db1[...], TN)

    kb = 256

    def att_back(p, _):
        stat = lse[p].T
        do = datt[p]
        q = q3[p]
        prod = (do.astype(F32) * att[p].astype(F32)).T
        keep = [lanes_of(j, length) for j in range(2)]
        dos = [jnp.where(keep[j], do, jnp.zeros_like(do)) for j in range(2)]
        qs = [jnp.where(keep[j], q, jnp.zeros_like(q)) for j in range(2)]
        inner = [
            jnp.sum(prod[HDIM * j : HDIM * j + HDIM, :], axis=0, keepdims=True) for j in range(2)
        ]
        dqs[...] = jnp.zeros_like(dqs)

        def keys(b, _):
            rows = pl.ds(pl.multiple_of(b * kb, kb), kb)
            k, v = k3[p, rows, :], v3[p, rows, :]
            dv, dk, dq = [], [], []
            for j in range(2):
                pt = jnp.exp(dot(k, qs[j], NT) - stat[j : j + 1, :])
                dst = (pt * (dot(v, dos[j], NT) - inner[j])).astype(BF16)
                dv.append(dot(pt.astype(BF16), dos[j]))
                dk.append(dot(dst, qs[j]))
                kj = jnp.where(lanes_of(j, kb), k, jnp.zeros_like(k))
                dq.append(dot(dst, kj, TN))
            dpj[2 * PAIRS + p, rows, :] = (dv[0] + dv[1]).astype(BF16)
            dpj[PAIRS + p, rows, :] = (dk[0] + dk[1]).astype(BF16)
            dqs[...] += dq[0] + dq[1]
            return 0

        lax.fori_loop(0, length // kb, keys, 0)
        dpj[p] = (dqs[...] * (HDIM**-0.5)).astype(BF16)
        return 0

    lax.fori_loop(0, PAIRS, att_back, 0)

    def last_tile(t, _):
        rows = pl.ds(pl.multiple_of(t * tile, tile), tile)
        dp = jnp.concatenate([dpj[c, rows, :] for c in range(3 * PAIRS)], axis=1)
        dn1 = dot(dp, w_qkv[...], NT)
        n1, r1 = normalise(lat[rows, :].astype(F32))
        latg_o[rows, :] = (dmid[rows, :] + norm_back(dn1 * scale1, n1, r1)).astype(BF16)
        acc[0, :, 0:D] += fold(dn1)
        acc[1, :, 0:D] += fold(dn1 * n1)
        acc[9, :, 0 : 3 * D] += fold(dp.astype(F32))
        return 0

    lax.fori_loop(0, tiles, last_tile, 0)
    for c in range(3):
        cols = jnp.concatenate([dpj[PAIRS * c + p] for p in range(PAIRS)], axis=1)
        gqkv_o[:, D * c : D * c + D] = dot(nm1[...], cols, TN)

    def total(i):
        return jnp.sum(acc[i], axis=0, keepdims=True)

    for i in range(6):
        dmod_o[i : i + 1, :] = total(i)[:, 0:D]
    bout_o[...] = total(6)[:, 0:D]
    bdown_o[...] = total(7)[:, 0:D]
    bup_o[...] = total(8)
    bqkv_o[...] = total(9)[:, 0 : 3 * D]


def block(lat, og, mod, weights, biases):
    length = lat.shape[0]
    row = lambda n: jax.ShapeDtypeStruct((1, n), F32)
    act = jax.ShapeDtypeStruct((length, D), BF16)
    mat = lambda r, c: jax.ShapeDtypeStruct((r, c), F32)
    vm = lambda *shape: pltpu.VMEM(shape, BF16)
    return pl.pallas_call(
        block_kernel,
        out_shape=(
            act, act, mat(D, 3 * D), mat(D, D), mat(D, FF), mat(FF, D),
            row(3 * D), row(D), row(FF), row(D), jax.ShapeDtypeStruct((6, D), F32),
        ),
        in_specs=[pl.BlockSpec(memory_space=pltpu.VMEM)] * 11,
        out_specs=[pl.BlockSpec(memory_space=pltpu.VMEM)] * 11,
        scratch_shapes=[
            vm(length, D), vm(PAIRS, length, 128), vm(PAIRS, length, 128), vm(PAIRS, length, 128),
            vm(PAIRS, length, 128), pltpu.VMEM((PAIRS, length, 128), F32), vm(PAIRS, length, 128),
            vm(3 * PAIRS, length, 128), pltpu.VMEM((length, 128), F32),
            vm(length, D), vm(length, FF), vm(length, FF), vm(length, D), vm(length, D),
            pltpu.VMEM((length, D), F32), pltpu.VMEM((10, 8, FF), F32),
        ],
        compiler_params=pltpu.CompilerParams(vmem_limit_bytes=60 << 20),
        name="block",
    )(lat, og, mod, *weights, *biases)


def local(
    latents, condition, out_grad, master, moment_one, moment_two, bias_master, bias_one, bias_two
):
    groups = lax.axis_size("grp")
    packed, bias_packed = (
        lax.all_gather(master.astype(BF16), "grp", axis=0, tiled=True),
        lax.all_gather(bias_master.astype(BF16), "grp", axis=0, tiled=True),
    )
    matrices, biases = unpack(packed, bias_packed, groups)
    w_ada = matrices[4]
    rows = [vector.astype(F32)[None, :] for vector in biases]
    cond_low = jax.nn.silu(condition).astype(BF16)
    modulation = jnp.dot(cond_low, w_ada, preferred_element_type=F32) + rows[4]
    (
        block_out, latent_grad, g_qkv, g_out, g_up, g_down, gb_qkv, gb_out, gb_up, gb_down, dmod,
    ) = block(latents, out_grad, modulation.reshape(6, D), matrices[:4], rows[:4])
    modulation_grad = dmod.reshape(1, 6 * D).astype(BF16)
    grad_ada = cond_low.T.astype(F32) * modulation_grad.astype(F32)
    grad_b_ada = modulation_grad.astype(F32)[0]
    silu_back = jax.vjp(jax.nn.silu, condition)[1]
    condition_grad = silu_back(jnp.dot(modulation_grad, w_ada.T, preferred_element_type=F32))[0]
    grad_pack, bias_pack = pack(
        [g_qkv, g_out, g_up, g_down, grad_ada],
        [gb_qkv[0], gb_out[0], gb_up[0], gb_down[0], grad_b_ada],
        groups,
    )
    summed, bias_summed = lax.psum((grad_pack, bias_pack), "rep")
    owned, bias_owned = (
        lax.psum_scatter(summed, "grp", scatter_dimension=0, tiled=True),
        lax.psum_scatter(bias_summed, "grp", scatter_dimension=0, tiled=True),
    )
    new_master, new_one, new_two, lamb_stats = lamb_step(
        master, moment_one, moment_two, owned, groups, norm_totals
    )
    new_bias, new_bias_one, new_bias_two = adam_step(bias_master, bias_one, bias_two, bias_owned)
    return (
        block_out,
        latent_grad,
        condition_grad,
        lamb_stats,
        new_master,
        new_one,
        new_two,
        new_master.astype(BF16),
        new_bias,
        new_bias_one,
        new_bias_two,
        new_bias.astype(BF16),
    )


def solution(mesh):
    row, own, vec = P(("rep", "grp"), None), P("grp", None), P("grp")
    return jax.shard_map(
        local,
        mesh=mesh,
        in_specs=(row, row, row, own, own, own, vec, vec, vec),
        out_specs=(row, row, row, P(), own, own, own, own, vec, vec, vec, vec),
        check_vma=False,
    )
```

```python
import math

import jax
import jax.numpy as jnp
from jax import lax
from jax.experimental import pallas as pl
from jax.experimental.pallas import tpu as pltpu
from jax.sharding import PartitionSpec as P

D = 384
FF = 1536
HEADS = 6
HDIM = 64
PAIRS = HEADS // 2

NORM_EPS = 1e-06
BETA_ONE = 0.5
BETA_TWO = 0.5
ADAM_EPS = 1e-06
STEP_RATE = 0.3
DECAY_RATE = 0.01

F32 = jnp.float32
BF16 = jnp.bfloat16
NN = ((1,), (0,))
NT = ((1,), (1,))
TN = ((0,), (0,))
GELU_A = 0.044715
GELU_C = 0.7978845608028654


def dot(a, b, dims=NN):
    return lax.dot_general(a, b, (dims, ((), ())), preferred_element_type=F32)


def matrix_shapes():
    return [(D, 3 * D), (D, D), (D, FF), (FF, D), (D, 6 * D)]


def bias_lengths():
    return [3 * D, D, FF, D, 6 * D]


def owner_extents(groups):
    return [row_count // groups * col_count for row_count, col_count in matrix_shapes()]


def mean_last(v):
    return jnp.sum(v, axis=-1, keepdims=True) * (1.0 / v.shape[-1])


def normalise(v):
    centered = v - mean_last(v)
    r = lax.rsqrt(mean_last(centered * centered) + NORM_EPS)
    return centered * r, r


def norm_back(e, n, r):
    return r * (e - mean_last(e) - n * mean_last(e * n))


def fold(v):
    return jnp.sum(v.reshape(v.shape[0] // 8, 8, v.shape[1]), axis=0)


def lanes_of(j, rows):
    lane = lax.broadcasted_iota(jnp.int32, (rows, 2 * HDIM), 1)
    return (lane >= HDIM) if j else (lane < HDIM)


def regions(groups):
    found, base = [], 0
    for (row_count, col_count), extent in zip(matrix_shapes(), owner_extents(groups)):
        found.append((base, extent // 128, col_count // 128, row_count // groups))
        base += extent // 128
    return found


class Chunk:
    def __init__(self, kind, name, stride, row0, rows, col0, cols, plan, pair=None):
        self.kind, self.name, self.stride, self.row0, self.rows = kind, name, stride, row0, rows
        self.col0, self.cols, self.pair, self.half, self.unit = col0, cols, pair, rows // 2, plan.unit
        self.slabs = rows * cols // (2 * plan.unit * 128)
        self.per = -(-self.slabs // plan.layers)
        self.sets = self.slabs // self.per
        self.direct = pair is not None

    def slab(self, s):
        tiles = self.cols // 128
        return self.unit * (s // tiles), 128 * (s % tiles)

    def tile(self, s):
        col = self.slab(s)[1] // 128
        return self.col0 // 128 + col if self.pair is None else col * PAIRS + self.pair


def adam(first, second, grad):
    first = BETA_ONE * first + (1.0 - BETA_ONE) * grad
    second = BETA_TWO * second + (1.0 - BETA_TWO) * grad * grad
    return first / (second * lax.rsqrt(second) + ADAM_EPS), first, second


class Plan:
    def __init__(self, groups, reps, length):
        self.groups, self.reps, self.length = groups, reps, length
        self.layers = reps // 2
        self.regions = regions(groups)
        self.rows = sum(r[1] for r in self.regions)
        part = D // groups
        self.unit = part // 2
        self.chunks = []
        for i in range(2):
            rows = FF // groups // 2
            self.chunks.append(Chunk(3, "gdown", FF // groups, rows * i, rows, 0, D, self))
        for i in range(2):
            self.chunks.append(Chunk(2, "gup", part, 0, part, FF // 2 * i, FF // 2, self))
        self.chunks.append(Chunk(1, "gout", part, 0, part, 0, D, self))
        for p in range(PAIRS):
            self.chunks.append(Chunk(0, "gq", part, 0, part, 0, D, self, p))
        self.biases = [n // groups for n in bias_lengths()]
        self.widths = [128 * groups + 4 * D + 2 * D + FF, 3 * D, 2 * D]


def scratch_of(plan):
    length, groups, layers = plan.length, plan.groups, plan.layers
    b = lambda *shape: pltpu.VMEM(shape, BF16)
    f = lambda *shape: pltpu.VMEM(shape, F32)
    dma = lambda *shape: pltpu.SemaphoreType.DMA(shape)
    n = len(plan.chunks)
    items = dict(
        lat=b(length, D), og=b(length, D),
        w_qkv=b(D, 3 * D), w_out=b(D, D), w_up=b(D, FF), w_down=b(FF, D), w_ada=b(D // groups, 6 * D),
        mst=f(plan.rows, 128), one=f(plan.rows, 128), two=f(plan.rows, 128), gpk=f(plan.rows, 128),
        act_s=f(groups, 1, 128), act_r=f(groups, 1, 128),
        mp_s=f(groups, 1, 6 * D), mp_r=f(groups, 1, 6 * D), mod=f(1, 6 * D),
        b_all=f(groups, 1, sum(plan.biases)), b_qkv=f(1, 3 * D), b_out=f(1, D), b_up=f(1, FF), b_down=f(1, D),
        nm1=b(length, D), q3=b(PAIRS, length, 128), k3=b(PAIRS, length, 128), v3=b(PAIRS, length, 128),
        att=b(PAIRS, length, 128), lse=f(PAIRS, 8, length), datt=b(PAIRS, length, 128),
        dpj=b(3 * PAIRS * length, 128), dqs=f(length, 128), stt=f(4, length),
        hid=b(length, FF), dhid=b(length, FF),
        dmid=f(length, D), acc=f(10, 8, FF),
        gdown=f(FF, D), gup=f(D, FF), gout=f(D, D), gq=f(PAIRS, D, D),
        rows2=f(32, 128 + 6 * D), brow=f(1, 6 * D + sum(bias_lengths()[:4])),
        bg=f(groups, 1, sum(plan.biases)),
        cg_s=f(groups, 1, 128), cg_r=f(groups, 1, 128), nrm=f(groups, 1, 128),
        ls=dma(16), ws=dma(6, 3), wr=dma(6, 3), ts=dma(5, 3), tr=dma(5, 3),
        es=dma(n, 2 * layers), cs=dma(n, 7), cr=dma(n, 7), xs=dma(3, 5), xr=dma(3, 5), os=dma(16), st=dma(5, 3),
    )
    for i, width in enumerate(plan.widths):
        items[f"row{i}"] = f(groups, 2, layers, 1, width)
    kinds = {BF16: b, F32: f}
    for k, one in enumerate(plan.chunks):
        items[f"ra{k}"] = f(2, one.rows, one.cols)
        items[f"sb{k}"] = b(one.rows, one.cols)
        items[f"rb{k}"] = b(one.rows, one.cols)
        if not one.direct:
            items[f"sc{k}"] = kinds[HALF_TYPE](one.half, one.cols)
            items[f"rc{k}"] = kinds[HALF_TYPE](one.half, one.cols)
        halves = 2 if one.direct else 1
        items[f"hf{k}"] = f(halves * one.slabs, plan.unit, 128)
        if LAYER_TYPE is not F32:
            items[f"sd{k}"] = b(halves * one.slabs, plan.unit, 128)
        items[f"rd{k}"] = kinds[LAYER_TYPE](halves * layers, one.per, plan.unit, 128)
        items[f"ag{k}"] = kinds[SPREAD_TYPE](2, one.slabs, plan.unit, 128)
    return items


HALF_TYPE, LAYER_TYPE, SPREAD_TYPE = BF16, BF16, BF16


def encode(value):
    return (value * jnp.abs(value)).astype(BF16)


def decode(code):
    wide = code.astype(F32)
    return wide * lax.rsqrt(jnp.maximum(jnp.abs(wide), 1e-37))


class Refs:
    def __init__(self, names, refs):
        for name, ref in zip(names, refs, strict=True):
            setattr(self, name, ref)


ARGS = ["lat_h", "og_h", "cond", "mst_h", "one_h", "two_h", "bm_h"]
OUTS = ["out_h", "latg_h", "gpk_h", "none_h", "ntwo_h", "back", "squares", "bgrad"]


def at(value, step):
    return pl.multiple_of(value, step)


def step_kernel(plan, names, *refs):
    v = Refs(ARGS + OUTS + names, refs)
    groups, reps, layers, length = plan.groups, plan.reps, plan.layers, plan.length
    r, g = lax.axis_index("rep"), lax.axis_index("grp")
    h, zi, c, x = r % 2, r // 2, g % 2, g // 2
    g1, g2, g3, r1 = g + 1 - 2 * c, g + 2 - 4 * x, 3 - g, r + 1 - 2 * h
    others = [g1, g2, g3]
    part = D // groups

    def rdma(src, dst, send, recv, rep, grp):
        return pltpu.make_async_remote_copy(
            src_ref=src, dst_ref=dst, send_sem=send, recv_sem=recv,
            device_id=(rep, grp), device_id_type=pl.DeviceIdType.MESH,
        )

    def layer_rep(dz):
        return ((zi + dz) % layers) * 2 + h

    barrier = pltpu.get_barrier_semaphore()

    def greet(rep, grp):
        pl.semaphore_signal(barrier, inc=1, device_id=(rep, grp), device_id_type=pl.DeviceIdType.MESH)

    for t in others:
        greet(r, t)

    def any_rep(d):
        return ((zi + d // 2) % layers) * 2 + (h + d) % 2

    def greet_rep(d, _):
        greet(any_rep(d), g)
        return 0

    lax.fori_loop(1, reps, greet_rep, 0)

    def region_copy(src, dst, k, sem):
        base, count, _, _ = plan.regions[k]
        return pltpu.make_async_copy(src.at[pl.ds(base, count), :], dst.at[pl.ds(base, count), :], sem)

    loads = [region_copy(v.mst_h, v.mst, k, v.ls.at[k]) for k in range(5)]
    for k in (0, 4):
        loads[k].start()
    lat_in = pltpu.make_async_copy(v.lat_h, v.lat, v.ls.at[5])
    og_in = pltpu.make_async_copy(v.og_h, v.og, v.ls.at[6])
    one_in = pltpu.make_async_copy(v.one_h, v.one, v.ls.at[7])
    two_in = pltpu.make_async_copy(v.two_h, v.two, v.ls.at[8])
    lat_in.start()
    for k in (1, 2, 3):
        loads[k].start()

    cond = v.cond[...]
    sig = 1.0 / (1.0 + jnp.exp(-cond))
    act = (cond * sig).astype(BF16).astype(F32)
    v.act_s[...] = jnp.zeros_like(v.act_s)
    for j in range(groups):
        v.act_s[j, :, 0:part] = act[:, part * j : part * j + part]
    v.b_all[g] = v.bm_h[...].reshape(1, sum(plan.biases)).astype(BF16).astype(F32)

    def own(k, dst, first, place=lambda t: t):
        base, _, tiles, rows = plan.regions[k]
        for i in range(rows // part):
            for t in range(tiles):
                piece = v.mst[pl.ds(base + part * i * tiles + t, part, stride=tiles), :]
                dst[pl.ds(at(first + part * i, 32), part), 128 * place(t) : 128 * place(t) + 128] = piece.astype(BF16)

    mats = [v.w_qkv] * PAIRS + [v.w_out, v.w_up, v.w_down]
    kinds = [0] * PAIRS + [1, 2, 3]

    def pair_place(t):
        return (t % PAIRS) * 3 + t // PAIRS

    def weight_copy(k, route):
        rows = plan.regions[kinds[k]][3]
        block, to = [(g, g1), (g, g2), (g2, g1)][route]
        where = pl.ds(at(block * rows, 32), rows)
        ref = mats[k].at[where, D * k : D * k + D] if k < PAIRS else mats[k].at[where, :]
        return rdma(ref, ref, v.ws.at[k, route], v.wr.at[k, route], r, to)

    loads[0].wait()
    own(0, v.w_qkv, g * part, pair_place)
    pl.semaphore_wait(barrier, 3 + reps - 1)

    def to_others(kind, src, dst):
        return [
            rdma(src(t), dst, v.ts.at[kind, i], v.tr.at[kind, i], r, t) for i, t in enumerate(others)
        ]

    act_out = to_others(0, lambda t: v.act_s.at[t], v.act_r.at[g])
    bias_out = to_others(1, lambda t: v.b_all.at[g], v.b_all.at[g])
    mod_out = to_others(2, lambda t: v.mp_s.at[t], v.mp_r.at[g])
    for copy in act_out:
        copy.start()
    weight_copy(0, 1).start()
    weight_copy(0, 0).start()
    v.act_r[g] = v.act_s[g]
    loads[4].wait()
    own(4, v.w_ada, 0)
    for copy in act_out:
        copy.wait_recv()
    left = jnp.concatenate([v.act_r[j][:, 0:part] for j in range(groups)] + [jnp.zeros((8 - groups, part), F32)], axis=0)
    parts = dot(left.astype(BF16), v.w_ada[...])
    for j in range(groups):
        v.mp_s[j] = parts[j : j + 1, :]
    for copy in mod_out:
        copy.start()
    v.mp_r[g] = v.mp_s[g]
    for p in range(1, PAIRS):
        weight_copy(p, 1).start()
        weight_copy(p, 0).start()
    for copy in bias_out:
        copy.start()
    og_in.start()
    for k in (1, 2, 3):
        loads[k].wait()
        own(k, mats[PAIRS - 1 + k], g * plan.regions[k][3])
        weight_copy(PAIRS - 1 + k, 1).start()
        weight_copy(PAIRS - 1 + k, 0).start()
        if k == 2:
            weight_copy(0, 1).wait_recv()
            weight_copy(0, 2).start()
    lat_in.wait()
    tile = 256
    tiles = length // tile

    def centre_tile(t, _):
        rows = pl.ds(at(t * tile, tile), tile)
        v.dmid[rows, :] = normalise(v.lat[rows, :].astype(F32))[0]
        return 0

    lax.fori_loop(0, tiles, centre_tile, 0)
    one_in.start()
    two_in.start()
    for copy in bias_out:
        copy.wait_recv()
    starts = [sum(plan.biases[:k]) for k in range(5)]

    def bias_row(k):
        s, n = starts[k], plan.biases[k]
        return jnp.concatenate([v.b_all[j][:, s : s + n] for j in range(groups)], axis=1)

    for k, ref in enumerate([v.b_qkv, v.b_out, v.b_up, v.b_down]):
        ref[...] = bias_row(k)
    flat = v.b_qkv[...]
    tiles_of = [flat[:, 128 * t : 128 * t + 128] for t in range(3 * PAIRS)]
    for t in range(3 * PAIRS):
        v.b_qkv[:, 128 * pair_place(t) : 128 * pair_place(t) + 128] = tiles_of[t]
    for copy in mod_out:
        copy.wait_recv()
    total = v.mp_r[0]
    for j in range(1, groups):
        total = total + v.mp_r[j]
    v.mod[...] = total + bias_row(4)

    def forward(k):
        weight_copy(k, 1).wait_recv()
        weight_copy(k, 2).start()

    def arrived(k):
        weight_copy(k, 0).wait_recv()
        weight_copy(k, 2).wait_recv()


    mod = v.mod
    shift1, scale1, gate1 = mod[:, 0:D], mod[:, D : 2 * D] + 1.0, mod[:, 2 * D : 3 * D]
    shift2, scale2, gate2 = mod[:, 3 * D : 4 * D], mod[:, 4 * D : 5 * D] + 1.0, mod[:, 5 * D : 6 * D]
    def norm_tile(t, _):
        rows = pl.ds(at(t * tile, tile), tile)
        v.nm1[rows, :] = (v.dmid[rows, :] * scale1 + shift1).astype(BF16)
        return 0

    lax.fori_loop(0, tiles, norm_tile, 0)

    def pair_cols(p):
        return pl.ds(at(p * D, D), D)

    def qkv_tile(p, t):
        rows = pl.ds(at(t * tile, tile), tile)
        proj = (dot(v.nm1[rows, :], v.w_qkv[:, pair_cols(p)]) + v.b_qkv[:, pair_cols(p)]).astype(BF16)
        v.q3[p, rows, :] = proj[:, 0:128] * jnp.asarray(HDIM**-0.5, BF16)
        v.k3[p, rows, :] = proj[:, 128:256]
        v.v3[p, rows, :] = proj[:, 256:384]

    qb = 256
    q_steps = length // qb

    def att_step(p, i):
        rows = pl.ds(at(i * qb, qb), qb)
        q = v.q3[p, rows, :]
        outs, stats = [], []
        for j in range(2):
            qj = jnp.where(lanes_of(j, qb), q, jnp.zeros_like(q))
            s = dot(qj, v.k3[p], NT)
            m = jnp.max(s, axis=-1, keepdims=True)
            e = jnp.exp(s - m)
            l = jnp.sum(e, axis=-1, keepdims=True)
            outs.append(dot((e * (1.0 / l)).astype(BF16), v.v3[p]))
            stats.append(m + jnp.log(l))
        v.att[p, rows, :] = jnp.where(lanes_of(0, qb), outs[0], outs[1]).astype(BF16)
        lane = lax.broadcasted_iota(jnp.int32, (qb, 128), 1)
        v.lse[p, :, rows] = jnp.where(lane == 0, stats[0], stats[1]).T[0:8, :]

    forwards = {(0, 0): [2], (0, 2): [3], (1, 2): [4], (2, 1): [5]}

    def att_pair(p, _):
        for k in range(PAIRS):
            @pl.when(p == k)
            def _(k=k):
                arrived(k)

        def project(t, _):
            qkv_tile(p, t)
            return 0

        lax.fori_loop(0, tiles, project, 0)

        @pl.when(p == 0)
        def _():
            forward(1)

        def attend(i, _):
            att_step(p, i)
            for (pp, ii), ks in forwards.items():
                @pl.when((p == pp) & (i == ii))
                def _(ks=ks):
                    for k in ks:
                        forward(k)
            return 0

        lax.fori_loop(0, q_steps, attend, 0)
        return 0

    lax.fori_loop(0, PAIRS, att_pair, 0)
    og_in.wait()
    for k in (3, 4, 5):
        arrived(k)

    acc = v.acc
    acc[...] = jnp.zeros_like(acc)

    def whole(i):
        return pl.ds(at(i * length, length), length)

    def spare_put(which, t, value):
        for i in range(PAIRS):
            v.dpj[pl.ds(at((which * PAIRS + i) * length + t * tile, tile), tile), :] = value[:, 128 * i : 128 * i + 128]

    def spare(which):
        return jnp.concatenate([v.dpj[whole(which * PAIRS + i), :] for i in range(PAIRS)], axis=1)

    def mlp_tile(t, _):
        rows = pl.ds(at(t * tile, tile), tile)
        atv = jnp.concatenate([v.att[p, rows, :] for p in range(PAIRS)], axis=1)
        branch1 = dot(atv, v.w_out[...]) + v.b_out[...]
        mid = v.lat[rows, :].astype(F32) + gate1 * branch1
        n2, r2 = normalise(mid)
        normed = (n2 * scale2 + shift2).astype(BF16)
        spare_put(0, t, normed)
        pre = dot(normed, v.w_up[...]) + v.b_up[...]
        sq = pre * pre
        th = jnp.tanh(pre * (GELU_C + (GELU_C * GELU_A) * sq))
        half = 0.5 + 0.5 * th
        hd = (pre * half).astype(BF16)
        v.hid[rows, :] = hd
        slope = half + (0.5 * pre) * (1.0 - th * th) * (GELU_C + (3.0 * GELU_C * GELU_A) * sq)
        branch2 = dot(hd, v.w_down[...]) + v.b_down[...]
        og = v.og[rows, :].astype(F32)
        v.og[rows, :] = (mid + gate2 * branch2).astype(BF16)
        d2 = (gate2 * og).astype(BF16)
        spare_put(1, t, d2)
        dh = (dot(d2, v.w_down[...], NT) * slope).astype(BF16)
        v.dhid[rows, :] = dh
        dn2 = dot(dh, v.w_up[...], NT)
        dm = og + norm_back(dn2 * scale2, n2, r2)
        v.dmid[rows, :] = dm
        d1 = (gate1 * dm).astype(BF16)
        spare_put(2, t, d1)
        da = dot(d1, v.w_out[...], NT).astype(BF16)
        for p in range(PAIRS):
            v.datt[p, rows, :] = da[:, 128 * p : 128 * p + 128]
        acc[2, :, 0:D] += fold(dm * branch1)
        acc[3, :, 0:D] += fold(dn2)
        acc[4, :, 0:D] += fold(dn2 * n2)
        acc[5, :, 0:D] += fold(og * branch2)
        acc[6, :, 0:D] += fold(d1.astype(F32))
        acc[7, :, 0:D] += fold(d2.astype(F32))
        acc[8, :, :] += fold(dh.astype(F32))
        return 0

    lax.fori_loop(0, tiles, mlp_tile, 0)
    out_copy = pltpu.make_async_copy(v.og, v.out_h, v.os.at[0])
    out_copy.start()

    def total_of(i, width):
        return jnp.sum(acc[i], axis=0, keepdims=True)[:, 0:width]

    def low_row(i):
        return total_of(i, D).astype(BF16).astype(F32)

    rowbufs = [v.row0, v.row1, v.row2]

    def row_put(n, pieces):
        ref, place = rowbufs[n].at[g, h, zi], 0
        for piece in pieces:
            ref[:, place : place + piece.shape[1]] = piece
            place += piece.shape[1]

    def row_copy(n, stage):
        ref = rowbufs[n]
        src, to = {
            1: (ref.at[g, h], (r1, g)), 2: (ref.at[g], (r, g2)), 3: (ref.at[g], (r, g1)), 4: (ref.at[g2], (r, g1)),
        }[stage]
        return rdma(src, src, v.xs.at[n, stage], v.xr.at[n, stage], *to)

    def row_wait(n, sems):
        few = rowbufs[n].at[g, h, pl.ds(0, layers - 1)]
        return pltpu.make_async_copy(few, few, sems.at[n, 0])

    def row_step(n, stage):
        if stage == 0:
            ref = rowbufs[n].at[g, h, zi]

            def send_row(dz, _):
                rdma(ref, ref, v.xs.at[n, 0], v.xr.at[n, 0], layer_rep(dz), g).start()
                return 0

            lax.fori_loop(1, layers, send_row, 0)
        elif stage == 1:
            row_wait(n, v.xr).wait()
            row_copy(n, 1).start()
        elif stage == 2:
            row_copy(n, 1).wait_recv()
            row_copy(n, 2).start()
            row_copy(n, 3).start()
        elif stage == 3:
            row_copy(n, 2).wait_recv()
            row_copy(n, 4).start()
        else:
            row_copy(n, 3).wait_recv()
            row_copy(n, 4).wait_recv()

    def row_sent(n):
        row_wait(n, v.xs).wait()
        for stage in (1, 2, 3, 4):
            row_copy(n, stage).wait_send()

    row_put(0, [v.act_s[j] for j in range(groups)] + [low_row(i) for i in range(2, 6)]
            + [total_of(6, D), total_of(8, FF), total_of(7, D)])
    row_step(0, 0)

    def grad_of(k):
        one = plan.chunks[k]
        return v.gq.at[one.pair] if one.pair is not None else getattr(v, one.name)

    def buf(k, *names):
        return [getattr(v, f"{name}{k}") for name in names]

    def copy_a(k, kk):
        one = plan.chunks[k]
        (ra,) = buf(k, "ra")
        rows = pl.ds(at((2 * kk + 1 - c) * one.stride + one.row0, 32), one.rows)
        src = grad_of(k).at[rows, one.col0 : one.col0 + one.cols]
        return rdma(src, ra.at[kk], v.cs.at[k, 5 + kk], v.cr.at[k, 5 + kk], r, g1)

    def copy_b(k):
        sb, rb = buf(k, "sb", "rb")
        return rdma(sb, rb, v.cs.at[k, 0], v.cr.at[k, 0], r, g2)

    def copy_c(k):
        sc, rc = buf(k, "sc", "rc")
        return rdma(sc, rc, v.cs.at[k, 1], v.cr.at[k, 1], r1, g)

    def copy_f(k):
        (ag,) = buf(k, "ag")
        return rdma(ag.at[h], ag.at[h], v.cs.at[k, 4], v.cr.at[k, 4], r1, g)

    def by_rows(rows, body):
        def run(i, _):
            body(at(i * plan.unit, 16))
            return 0

        lax.fori_loop(0, rows // plan.unit, run, 0)

    def rows_at(value):
        return pl.ds(at(value, 16), plan.unit)

    def s1(k):
        for kk in range(2):
            copy_a(k, kk).start()

    def s2(k):
        one = plan.chunks[k]
        ra, sb = buf(k, "ra", "sb")
        for kk in range(2):
            copy_a(k, kk).wait_recv()
        first = (2 * (1 - x) + c) * one.stride + one.row0
        cols = slice(one.col0, one.col0 + one.cols)

        def body(i):
            sb[rows_at(i), :] = encode(grad_of(k)[rows_at(first + i), cols] + ra[1 - x, rows_at(i), :])

        by_rows(one.rows, body)
        copy_b(k).start()

    def s3(k):
        one = plan.chunks[k]
        ra, rb, sc = buf(k, "ra", "rb", "sc")
        copy_b(k).wait_recv()
        first = (1 - h) * one.half
        cols = slice(one.col0, one.col0 + one.cols)

        def body(i):
            mine = grad_of(k)[rows_at(g * one.stride + one.row0 + first + i), cols]
            total = mine + ra[x, rows_at(first + i), :] + decode(rb[rows_at(first + i), :])
            sc[rows_at(i), :] = encode(total)

        by_rows(one.half, body)
        copy_c(k).start()

    def set_at(k, q):
        return pl.ds(q * plan.chunks[k].per, plan.chunks[k].per)

    def sent_slabs(k):
        return buf(k, "hf")[0] if LAYER_TYPE is F32 else buf(k, "sd")[0]

    def copy_d(k, q, to):
        (rd,) = buf(k, "rd")
        slot = (zi - to + layers) % layers
        return rdma(sent_slabs(k).at[set_at(k, q)], rd.at[slot], v.cs.at[k, 2], v.cr.at[k, 2], to * 2 + h, g)

    def s4(k):
        one = plan.chunks[k]
        ra, rb, rc, hf = buf(k, "ra", "rb", "rc", "hf")
        copy_c(k).wait_recv()
        first = h * one.half
        for s in range(one.slabs):
            i, col = one.slab(s)
            cols = slice(col, col + 128)
            near = pl.ds(at(first + i, 16), plan.unit)
            mine = grad_of(k)[rows_at(g * one.stride + one.row0 + first + i), one.col0 + col : one.col0 + col + 128]
            far = decode(rb[near, cols]) + decode(rc[i : i + plan.unit, cols])
            value = mine + ra[x, near, cols] + far
            hf[s] = value
            if LAYER_TYPE is not F32:
                buf(k, "sd")[0][s] = encode(value)
        for q in range(one.sets):
            to = (q + k) % layers

            @pl.when(to != zi)
            def _(q=q, to=to):
                copy_d(k, q, to).start()

    def mine_of(k):
        return (zi - k % layers + layers) % layers

    def slab_bytes(k, count, sem, name):
        if name == "ag":
            ref = buf(k, "ag")[0].at[0, pl.ds(0, count * plan.chunks[k].per)]
        else:
            ref = buf(k, "rd")[0].at[pl.ds(0, count)]
        return pltpu.make_async_copy(ref, ref, sem)

    def copy_e(k, q, dz):
        (ag,) = buf(k, "ag")
        ref = ag.at[h, set_at(k, q)]
        return rdma(ref, ref, v.es.at[k, dz], v.cr.at[k, 3], layer_rep(dz), g)

    def s5(k):
        one = plan.chunks[k]
        hf, rd, ag = buf(k, "hf", "rd", "ag")
        q, per = mine_of(k), one.per

        @pl.when(q < one.sets)
        def _():
            slab_bytes(k, layers - 1, v.cr.at[k, 2], "rd").wait()
            for i in range(per):
                def add(z, value):
                    return value + decode(rd[z, i])

                value = lax.fori_loop(1, layers, add, hf[q * per + i], unroll=layers <= 4)
                ag[h, q * per + i] = encode(value)

            def send(dz, _):
                copy_e(k, q, dz).start()
                return 0

            lax.fori_loop(1, layers, send, 0)

    def s6(k):
        sets = plan.chunks[k].sets

        @pl.when(mine_of(k) < sets)
        def _():
            slab_bytes(k, sets - 1, v.cr.at[k, 3], "ag").wait()

        @pl.when(mine_of(k) >= sets)
        def _():
            slab_bytes(k, sets, v.cr.at[k, 3], "ag").wait()

        copy_f(k).start()

    def s7(k):
        copy_f(k).wait_recv()
        unpack(k)

    def unpack(k):
        one = plan.chunks[k]
        (ag,) = buf(k, "ag")
        base, _, across, _ = plan.regions[one.kind]
        for half in range(2):
            for s in range(one.slabs):
                first = base + (one.row0 + half * one.half + one.slab(s)[0]) * across + one.tile(s)
                v.gpk[pl.ds(first, plan.unit, stride=across), :] = decode(ag[half, s])

    def sent(k):
        sets = plan.chunks[k].sets
        for kk in range(0 if k in (2, 3) else 2):
            copy_a(k, kk).wait_send()
        copy_b(k).wait_send()
        copy_c(k).wait_send()
        copy_f(k).wait_send()

        @pl.when(mine_of(k) < sets)
        def _():
            slab_bytes(k, sets - 1, v.cs.at[k, 2], "rd").wait()
            spread(k, layers - 1)

        @pl.when(mine_of(k) >= sets)
        def _():
            slab_bytes(k, sets, v.cs.at[k, 2], "rd").wait()

    def spread(k, count):
        def wait(dz, _):
            copy_e(k, mine_of(k), dz).wait_send()
            return 0

        lax.fori_loop(1, 1 + count, wait, 0)

    def direct_out(k, hh, q):
        sd, rd = buf(k, "sd", "rd")
        to = (q + k) % layers
        slot = ((zi - to + layers) % layers) * 2 + (h - hh) % 2
        src = sd.at[pl.ds((hh * plan.chunks[k].sets + q) * plan.chunks[k].per, plan.chunks[k].per)]
        return rdma(src, rd.at[slot], v.cs.at[k, 2], v.cr.at[k, 2], to * 2 + hh, g)

    def direct_back(k, d):
        (ag,) = buf(k, "ag")
        ref = ag.at[h, set_at(k, mine_of(k))]
        return rdma(ref, ref, v.es.at[k, d], v.cr.at[k, 3], any_rep(d), g)

    def d3(k):
        one = plan.chunks[k]
        ra, rb, hf, sd = buf(k, "ra", "rb", "hf", "sd")
        copy_b(k).wait_recv()
        for hh in range(2):
            for s in range(one.slabs):
                i, col = one.slab(s)
                i = i + hh * one.half
                cols = slice(col, col + 128)
                mine = grad_of(k)[rows_at(g * one.stride + one.row0 + i), one.col0 + col : one.col0 + col + 128]
                value = mine + ra[x, i : i + plan.unit, cols] + decode(rb[i : i + plan.unit, cols])
                hf[hh * one.slabs + s] = value
                sd[hh * one.slabs + s] = encode(value)
        for hh in range(2):
            for q in range(one.sets):
                @pl.when(((q + k) % layers != zi) | (hh != h))
                def _(hh=hh, q=q):
                    direct_out(k, hh, q).start()

    def d5(k):
        one = plan.chunks[k]
        hf, rd, ag = buf(k, "hf", "rd", "ag")
        q, per = mine_of(k), one.per

        @pl.when(q < one.sets)
        def _():
            slab_bytes(k, reps - 1, v.cr.at[k, 2], "rd").wait()
            for i in range(per):
                def add(d, value):
                    return value + decode(rd[d, i])

                value = lax.fori_loop(1, reps, add, hf[h * one.slabs + q * per + i], unroll=reps <= 8)
                ag[h, q * per + i] = encode(value)

            def send(d, _):
                direct_back(k, d).start()
                return 0

            lax.fori_loop(1, reps, send, 0)

    def d7(k):
        sets = plan.chunks[k].sets

        @pl.when(mine_of(k) < sets)
        def _():
            slab_bytes(k, 2 * sets - 1, v.cr.at[k, 3], "rd").wait()

        @pl.when(mine_of(k) >= sets)
        def _():
            slab_bytes(k, 2 * sets, v.cr.at[k, 3], "rd").wait()

        unpack(k)

    def direct_sent(k):
        sets = plan.chunks[k].sets
        for kk in range(2):
            copy_a(k, kk).wait_send()
        copy_b(k).wait_send()

        @pl.when(mine_of(k) < sets)
        def _():
            slab_bytes(k, 2 * sets - 1, v.cs.at[k, 2], "rd").wait()

            def wait(d, _):
                direct_back(k, d).wait_send()
                return 0

            lax.fori_loop(1, reps, wait, 0)

        @pl.when(mine_of(k) >= sets)
        def _():
            slab_bytes(k, 2 * sets, v.cs.at[k, 2], "rd").wait()

    direct_steps = {"1": s1, "2": s2, "3": d3, "5": d5, "7": d7}
    steps = dict(zip("1234567", (s1, s2, s3, s4, s5, s6, s7)))

    def run(text):
        for word in text:
            if word[0] == "r":
                row_step(int(word[1]), int(word[2]))
            else:
                k = int(word[1])
                (direct_steps if plan.chunks[k].direct else steps)[word[0]](k)

    def stores(k):
        pairs = ((v.gpk, v.gpk_h), (v.one, v.none_h), (v.two, v.ntwo_h))
        return [region_copy(a, b, k, v.st.at[k, i]) for i, (a, b) in enumerate(pairs)]

    def lamb(k):
        base, count, _, _ = plan.regions[k]

        size = 288

        def body(i, sums):
            rows = pl.ds(at(base + i * size, 32), size)
            grad, w = v.gpk[rows, :], v.mst[rows, :]
            move, v.one[rows, :], v.two[rows, :] = adam(v.one[rows, :], v.two[rows, :], grad)
            update = move + DECAY_RATE * w
            v.gpk[rows, :] = update
            return sums[0] + fold(w * w), sums[1] + fold(update * update)

        zero = jnp.zeros((8, 128), F32)
        sums = lax.fori_loop(0, count // size, body, (zero, zero))
        for copy in stores(k):
            copy.start()
        return [jnp.sum(jnp.sum(one, axis=1, keepdims=True), axis=0, keepdims=True) for one in sums]

    def g_down(i, _):
        cols = pl.ds(at(i * D, D), D)
        v.gdown[cols, :] = dot(v.hid[:, cols], spare(1), TN)
        return 0

    def g_up(i, _):
        cols = pl.ds(at(i * D, D), D)
        v.gup[:, cols] = dot(spare(0), v.dhid[:, cols], TN)
        return 0

    lax.fori_loop(0, FF // D, g_down, 0)
    run(["10", "11", "r01"])
    lax.fori_loop(0, FF // D // 2, g_up, 0)
    run(["20", "12"])
    lax.fori_loop(FF // D // 2, FF // D, g_up, 0)
    run(["21", "13"])
    for p in range(PAIRS):
        v.gout[128 * p : 128 * p + 128, :] = dot(v.att[p], spare(2), TN)
    run(["22", "14"])

    kb = 256
    k_steps = length // kb
    after = {
        0: ["23", "24"], 2: ["30"], 3: ["15", "31"], 4: ["25", "32", "40"], 5: ["33", "r02"],
        6: ["34", "41", "42"], 7: ["16", "35", "43", "50"], 8: ["26", "44", "51"],
        9: ["52", "55", "r03"], 10: ["53", "60"], 11: ["17", "36", "61", "62", "54"],
    }

    def att_back(it, _):
        p, b = it // k_steps, it % k_steps
        do, q = v.datt[p], v.q3[p]

        @pl.when(b == 0)
        def _():
            prod = (do.astype(F32) * v.att[p].astype(F32)).T
            v.stt[0:2, :] = v.lse[p, 0:2, :]
            for j in range(2):
                v.stt[2 + j : 3 + j, :] = jnp.sum(prod[HDIM * j : HDIM * j + HDIM, :], axis=0, keepdims=True)
            v.dqs[...] = jnp.zeros_like(v.dqs)

        rows = pl.ds(at(b * kb, kb), kb)
        kk, vv = v.k3[p, rows, :], v.v3[p, rows, :]
        dv, dk, dq = [], [], []
        for j in range(2):
            keep = lanes_of(j, length)
            dos = jnp.where(keep, do, jnp.zeros_like(do))
            qs = jnp.where(keep, q, jnp.zeros_like(q))
            pt = jnp.exp(dot(kk, qs, NT) - v.stt[j : j + 1, :])
            dst = (pt * (dot(vv, dos, NT) - v.stt[2 + j : 3 + j, :])).astype(BF16)
            dv.append(dot(pt.astype(BF16), dos))
            dk.append(dot(dst, qs))
            kj = jnp.where(lanes_of(j, kb), kk, jnp.zeros_like(kk))
            dq.append(dot(dst, kj, TN))
        v.dpj[pl.ds(at((2 * PAIRS + p) * length + b * kb, kb), kb), :] = (dv[0] + dv[1]).astype(BF16)
        v.dpj[pl.ds(at((PAIRS + p) * length + b * kb, kb), kb), :] = (dk[0] + dk[1]).astype(BF16)
        v.dqs[...] += dq[0] + dq[1]

        @pl.when(b == k_steps - 1)
        def _():
            v.dpj[whole(p), :] = (v.dqs[...] * (HDIM**-0.5)).astype(BF16)
            cols = jnp.concatenate([v.dpj[whole(i * PAIRS + p), :] for i in range(3)], axis=1)
            v.gq[p] = dot(v.nm1[...], cols, TN)
            acc[9, :, pair_cols(p)] = fold(cols.astype(F32))

        for i, text in after.items():
            @pl.when(it == i)
            def _(text=text):
                run(text)
        return 0

    lax.fori_loop(0, PAIRS * k_steps, att_back, 0)

    row_put(1, [total_of(9, 3 * D)])
    row_step(1, 0)

    for k in (2, 3):
        for kk in range(2):
            copy_a(k, kk).wait_send()

    def last_tile(t, _):
        rows = pl.ds(at(t * tile, tile), tile)
        order = [k * PAIRS + p for p in range(PAIRS) for k in range(3)]
        dp = jnp.concatenate([v.dpj[pl.ds(at(i * length + t * tile, tile), tile), :] for i in order], axis=1)
        dn1 = dot(dp, v.w_qkv[...], NT)
        n1, _r = normalise(v.lat[rows, :].astype(F32))
        v.gup[0:tile, pair_cols(t)] = dn1
        acc[0, :, 0:D] += fold(dn1)
        acc[1, :, 0:D] += fold(dn1 * n1)
        for i, text in {0: ["27", "70", "r04"], 1: ["r11", "63"], 2: ["75"], 3: ["71", "72", "r12", "64", "56"]}.items():
            @pl.when(t == i)
            def _(text=text):
                run(text)
        return 0

    lax.fori_loop(0, tiles, last_tile, 0)
    row_put(2, [low_row(0), low_row(1)])
    run(["r20", "37"])

    def latent_tile(t, _):
        rows = pl.ds(at(t * tile, tile), tile)
        n1, rs1 = normalise(v.lat[rows, :].astype(F32))
        v.lat[rows, :] = (v.dmid[rows, :] + norm_back(v.gup[0:tile, pair_cols(t)] * scale1, n1, rs1)).astype(BF16)
        return 0

    lax.fori_loop(0, tiles, latent_tile, 0)
    latg_copy = pltpu.make_async_copy(v.lat, v.latg_h, v.os.at[11])
    latg_copy.start()

    one_in.wait()
    two_in.wait()
    sums = [None] * 5
    run(["r21", "r13"])
    sums[3] = lamb(3)
    run(["73"])
    sums[2] = lamb(2)
    run(["57", "r22", "r14", "74"])
    sums[1] = lamb(1)
    run(["76", "r23", "77", "r24"])

    m0 = 128 * groups
    base, _, across, _ = plan.regions[4]
    v.brow[...] = jnp.zeros_like(v.brow)

    def rows_of(n, _):
        sums = v.brow[...]
        for i in range(32):
            j = n * 32 + i
            early, mid, late = [ref.at[j // (2 * layers), (j // layers) % 2, j % layers] for ref in rowbufs]
            v.rows2[i : i + 1, 0:128] = early[:, pl.ds(at(g * 128, 128), 128)]
            dmod = jnp.concatenate([late[...], early[:, m0 : m0 + 4 * D]], axis=1)
            v.rows2[i : i + 1, 128:] = dmod
            sums = sums + jnp.concatenate([dmod, mid[...], early[:, m0 + 4 * D :]], axis=1)
        v.brow[...] = sums
        acts = v.rows2[:, 0:128].astype(BF16)
        for t in range(across):
            piece = dot(acts, v.rows2[:, 128 * t + 128 : 128 * t + 256].astype(BF16), TN)[0:part, :]
            rows = pl.ds(base + t, part, stride=across)
            v.gpk[rows, :] = v.gpk[rows, :] + piece
        return 0

    v.gpk[base : base + part * across, :] = jnp.zeros((part * across, 128), F32)
    lax.fori_loop(0, reps * groups // 32, rows_of, 0)

    dm4 = jnp.concatenate(
        [
            jnp.concatenate([v.row2[j, h, zi], v.row0[j, h, zi][:, m0 : m0 + 4 * D]], axis=1) for j in range(groups)
        ] + [jnp.zeros((8 - groups, 6 * D), F32)], axis=0
    )
    dact = dot(dm4.astype(BF16), v.w_ada[...], NT)
    v.cg_s[...] = jnp.zeros_like(v.cg_s)
    for j in range(groups):
        v.cg_s[j, :, 0:part] = dact[j : j + 1, :]
    cg_out = to_others(3, lambda t: v.cg_s.at[t], v.cg_r.at[g])
    for copy in cg_out:
        copy.start()
    v.cg_r[g] = v.cg_s[g]

    sums[4] = lamb(4)
    sums[0] = lamb(0)
    lane = lax.broadcasted_iota(jnp.int32, (1, 128), 1)
    packed = jnp.zeros((1, 128), F32)
    for k in range(5):
        packed = jnp.where(lane == k, sums[k][0], packed)
        packed = jnp.where(lane == 8 + k, sums[k][1], packed)
    v.nrm[g] = packed
    nrm_out = to_others(4, lambda t: v.nrm.at[g], v.nrm.at[g])
    for copy in nrm_out:
        copy.start()

    sumrow = v.brow[...]
    flat = sumrow[:, 6 * D : 9 * D]
    qkv_row = jnp.concatenate(
        [flat[:, 128 * pair_place(t) : 128 * pair_place(t) + 128] for t in range(3 * PAIRS)], axis=1
    )
    rest = sumrow[:, 9 * D :]
    grads_of = [qkv_row, rest[:, 0:D], rest[:, D : D + FF], rest[:, D + FF :], sumrow[:, 0 : 6 * D]]
    for j in range(groups):
        v.bg[j] = jnp.concatenate([one[:, n * j : n * j + n] for one, n in zip(grads_of, plan.biases)], axis=1)
    v.bgrad[...] = v.bg[g]

    for copy in cg_out:
        copy.wait_recv()
    back = jnp.concatenate([v.cg_r[j][:, 0:part] for j in range(groups)], axis=1)
    v.back[...] = back

    for copy in nrm_out:
        copy.wait_recv()
    squares = v.nrm[0]
    for j in range(1, groups):
        squares = squares + v.nrm[j]
    v.squares[...] = squares

    for k in range(6):
        for route in range(3):
            weight_copy(k, route).wait_send()
    for copy in act_out + bias_out + mod_out + cg_out + nrm_out:
        copy.wait_send()
    for k, one in enumerate(plan.chunks):
        (direct_sent if one.direct else sent)(k)
    for n in range(3):
        row_sent(n)
    out_copy.wait()
    latg_copy.wait()
    for k in range(5):
        for copy in stores(k):
            copy.wait()


def finish_kernel(plan, refs_in, refs_out, scratch):
    out_i, latg_i, upd, one, two, back, squares, bgrad, cond, mst, bm, b1, b2 = refs_in
    out_o, latg_o, condg, stats, nmst, none, ntwo, ncpy, nb, nb1, nb2, nbc = refs_out
    upd_v, mst_v, one_v, two_v, cpy_v, out_v, latg_v, scales, sem_in, sem_out, sem_b = scratch
    size = plan.regions[0][1]
    blocks = plan.rows // size

    def part(i):
        return pl.ds(at(i * size, 32), size)

    def load(i):
        pairs = ((upd, upd_v), (mst, mst_v))
        return [pltpu.make_async_copy(a.at[part(i), :], b.at[part(i), :], sem_in.at[i, n]) for n, (a, b) in enumerate(pairs)]

    def store(i):
        pairs = ((mst_v, nmst), (cpy_v, ncpy))
        return [pltpu.make_async_copy(a.at[part(i), :], b.at[part(i), :], sem_out.at[i, n]) for n, (a, b) in enumerate(pairs)]

    moves = [(one, one_v, none), (two, two_v, ntwo), (out_i, out_v, out_o), (latg_i, latg_v, latg_o)]
    arrive = [pltpu.make_async_copy(a, b, sem_b.at[n]) for n, (a, b, _c) in enumerate(moves)]
    leave = [pltpu.make_async_copy(b, d, sem_b.at[4 + n]) for n, (_a, b, d) in enumerate(moves)]
    for copy in arrive[0:1]:
        copy.start()
    for i in range(blocks):
        for copy in load(i):
            copy.start()
    for copy in arrive[1:]:
        copy.start()

    norms = jnp.sqrt(squares[...])
    weight_norm, update_norm = norms[:, 0:5], norms[:, 8:13]
    ratio = weight_norm / (update_norm + NORM_EPS)
    stats[0:1, :] = weight_norm
    stats[1:2, :] = update_norm
    stats[2:3, :] = ratio
    for k in range(5):
        scales[k] = jnp.broadcast_to(ratio[:, k : k + 1], (8, 128))
    sig = 1.0 / (1.0 + jnp.exp(-cond[...]))
    condg[...] = back[...] * (sig * (1.0 + cond[...] * (1.0 - sig)))
    move, first, second = adam(b1[...], b2[...], bgrad[...].reshape(bm.shape))
    fresh = bm[...] - STEP_RATE * move
    nb[...] = fresh
    nb1[...] = first
    nb2[...] = second
    nbc[...] = fresh.astype(BF16)

    arrive[0].wait()
    leave[0].start()
    edges = [base for base, _, _, _ in plan.regions] + [plan.rows]
    for i in range(blocks):
        for copy in load(i):
            copy.wait()
        for k in range(5):
            low, high = max(edges[k], i * size), min(edges[k + 1], (i + 1) * size)
            if low < high:
                scale = jnp.broadcast_to(scales[k][0:1, :], (96, 128))

                def apply(n, _, low=low, scale=scale):
                    rows = pl.ds(at(low + n * 96, 32), 96)
                    value = mst_v[rows, :] - STEP_RATE * (scale * upd_v[rows, :])
                    mst_v[rows, :] = value
                    cpy_v[rows, :] = value.astype(BF16)
                    return 0

                lax.fori_loop(0, (high - low) // 96, apply, 0)
        for copy in store(i):
            copy.start()
    for n in (1, 2, 3):
        arrive[n].wait()
        leave[n].start()
    for copy in leave:
        copy.wait()
    for i in range(blocks):
        for copy in store(i):
            copy.wait()


def local(
    latents, condition, out_grad, master, moment_one, moment_two, bias_master, bias_one, bias_two
):
    groups, reps = lax.axis_size("grp"), lax.axis_size("rep")
    plan = Plan(groups, reps, latents.shape[0])
    items = scratch_of(plan)
    names = list(items)
    sds = jax.ShapeDtypeStruct
    full = lambda dtype: sds(master.shape, dtype)
    count = bias_master.shape[0]
    act = sds(latents.shape, BF16)
    hbm, vmem = pl.BlockSpec(memory_space=pl.ANY), pl.BlockSpec(memory_space=pltpu.VMEM)
    held = pl.pallas_call(
        lambda *refs: step_kernel(plan, names, *refs),
        out_shape=(act, act, full(F32), full(F32), full(F32), sds((1, D), F32), sds((1, 128), F32), sds((1, count), F32)),
        in_specs=[hbm, hbm, vmem, hbm, hbm, hbm, vmem],
        out_specs=[hbm] * 5 + [vmem] * 3,
        scratch_shapes=list(items.values()),
        compiler_params=pltpu.CompilerParams(
            vmem_limit_bytes=67043328, collective_id=0, has_side_effects=True
        ),
        name="step",
    )(latents, out_grad, condition, master, moment_one, moment_two, bias_master)
    blocks = plan.rows // plan.regions[0][1]
    line = lambda dtype: sds((count,), dtype)
    f = lambda *shape: pltpu.VMEM(shape, F32)
    return pl.pallas_call(
        lambda *refs: finish_kernel(plan, refs[:13], refs[13:25], refs[25:]),
        out_shape=(
            act, act, sds(condition.shape, F32), sds((3, 5), F32),
            full(F32), full(F32), full(F32), full(BF16), line(F32), line(F32), line(F32), line(BF16),
        ),
        in_specs=[hbm] * 5 + [vmem] * 4 + [hbm] + [vmem] * 3,
        out_specs=[hbm, hbm, vmem, vmem, hbm, hbm, hbm, hbm, vmem, vmem, vmem, vmem],
        scratch_shapes=[
            f(plan.rows, 128), f(plan.rows, 128), f(plan.rows, 128), f(plan.rows, 128),
            pltpu.VMEM((plan.rows, 128), BF16), pltpu.VMEM(latents.shape, BF16), pltpu.VMEM(latents.shape, BF16),
            f(5, 8, 128), pltpu.SemaphoreType.DMA((blocks, 2)), pltpu.SemaphoreType.DMA((blocks, 2)),
            pltpu.SemaphoreType.DMA((8,)),
        ],
        compiler_params=pltpu.CompilerParams(vmem_limit_bytes=67043328),
        name="finish",
    )(*held, condition, master, bias_master, bias_one, bias_two)


def solution(mesh):
    row, own, vec = P(("rep", "grp"), None), P("grp", None), P("grp")
    return jax.shard_map(
        local,
        mesh=mesh,
        in_specs=(row, row, row, own, own, own, vec, vec, vec),
        out_specs=(row, row, row, P(), own, own, own, own, vec, vec, vec, vec),
        check_vma=False,
    )
```

```python
import math

import jax
import jax.numpy as jnp
from jax import lax
from jax.experimental import pallas as pl
from jax.experimental.pallas import tpu as pltpu
from jax.sharding import PartitionSpec as P

D = 384
FF = 1536
HEADS = 6
HDIM = 64
PAIRS = HEADS // 2

NORM_EPS = 1e-06
BETA_ONE = 0.5
BETA_TWO = 0.5
ADAM_EPS = 1e-06
STEP_RATE = 0.3
DECAY_RATE = 0.01

F32 = jnp.float32
BF16 = jnp.bfloat16
NN = ((1,), (0,))
NT = ((1,), (1,))
TN = ((0,), (0,))
GELU_A = 0.044715
GELU_C = 0.7978845608028654


def dot(a, b, dims=NN):
    return lax.dot_general(a, b, (dims, ((), ())), preferred_element_type=F32)


def matrix_shapes():
    return [(D, 3 * D), (D, D), (D, FF), (FF, D), (D, 6 * D)]


def bias_lengths():
    return [3 * D, D, FF, D, 6 * D]


def owner_extents(groups):
    return [row_count // groups * col_count for row_count, col_count in matrix_shapes()]


def mean_last(v):
    return jnp.sum(v, axis=-1, keepdims=True) * (1.0 / v.shape[-1])


def normalise(v):
    centered = v - mean_last(v)
    r = lax.rsqrt(mean_last(centered * centered) + NORM_EPS)
    return centered * r, r


def norm_back(e, n, r):
    return r * (e - mean_last(e) - n * mean_last(e * n))


def fold(v):
    return jnp.sum(v.reshape(v.shape[0] // 8, 8, v.shape[1]), axis=0)


def lanes_of(j, rows):
    lane = lax.broadcasted_iota(jnp.int32, (rows, 2 * HDIM), 1)
    return (lane >= HDIM) if j else (lane < HDIM)


def regions(groups):
    found, base = [], 0
    for (row_count, col_count), extent in zip(matrix_shapes(), owner_extents(groups)):
        found.append((base, extent // 128, col_count // 128, row_count // groups))
        base += extent // 128
    return found


class Chunk:
    def __init__(self, kind, name, stride, row0, rows, col0, cols, plan, pair=None):
        self.kind, self.name, self.stride, self.row0, self.rows = kind, name, stride, row0, rows
        self.col0, self.cols, self.pair, self.half, self.unit = col0, cols, pair, rows // 2, plan.unit
        self.slabs = rows * cols // (2 * plan.unit * 128)
        self.per = -(-self.slabs // plan.layers)
        self.sets = self.slabs // self.per
        self.direct = pair is not None

    def slab(self, s):
        tiles = self.cols // 128
        return self.unit * (s // tiles), 128 * (s % tiles)

    def tile(self, s):
        col = self.slab(s)[1] // 128
        return self.col0 // 128 + col if self.pair is None else col * PAIRS + self.pair


def adam(first, second, grad):
    first = BETA_ONE * first + (1.0 - BETA_ONE) * grad
    second = BETA_TWO * second + (1.0 - BETA_TWO) * grad * grad
    return first / (second * lax.rsqrt(second) + ADAM_EPS), first, second


class Plan:
    def __init__(self, groups, reps, length):
        self.groups, self.reps, self.length = groups, reps, length
        self.layers = reps // 2
        self.regions = regions(groups)
        self.rows = sum(r[1] for r in self.regions)
        part = D // groups
        self.unit = part // 2
        self.chunks = []
        for i in range(2):
            rows = FF // groups // 2
            self.chunks.append(Chunk(3, "gdown", FF // groups, rows * i, rows, 0, D, self))
        for i in range(2):
            self.chunks.append(Chunk(2, "gup", part, 0, part, FF // 2 * i, FF // 2, self))
        self.chunks.append(Chunk(1, "gout", part, 0, part, 0, D, self))
        for p in range(PAIRS):
            self.chunks.append(Chunk(0, "gq", part, 0, part, 0, D, self, p))
        self.biases = [n // groups for n in bias_lengths()]
        self.widths = [128 * groups + 4 * D + 2 * D + FF, 3 * D, 2 * D]


def scratch_of(plan):
    length, groups, layers = plan.length, plan.groups, plan.layers
    b = lambda *shape: pltpu.VMEM(shape, BF16)
    f = lambda *shape: pltpu.VMEM(shape, F32)
    dma = lambda *shape: pltpu.SemaphoreType.DMA(shape)
    n = len(plan.chunks)
    items = dict(
        lat=b(length, D), og=b(length, D),
        w_qkv=b(D, 3 * D), w_out=b(D, D), w_up=b(D, FF), w_down=b(FF, D), w_ada=b(D // groups, 6 * D),
        mst=f(plan.rows, 128), one=f(plan.rows, 128), two=f(plan.rows, 128), gpk=f(plan.rows, 128),
        act_s=f(groups, 1, 128), act_r=f(groups, 1, 128),
        mp_s=f(groups, 1, 6 * D), mp_r=f(groups, 1, 6 * D), mod=f(1, 6 * D),
        b_all=f(groups, 1, sum(plan.biases)), b_qkv=f(1, 3 * D), b_out=f(1, D), b_up=f(1, FF), b_down=f(1, D),
        nm1=b(length, D), q3=b(PAIRS, length, 128), k3=b(PAIRS, length, 128), v3=b(PAIRS, length, 128),
        att=b(PAIRS, length, 128), lse=f(PAIRS, 8, length), datt=b(PAIRS, length, 128),
        dpj=b(3 * PAIRS * length, 128), dqs=f(length, 128), stt=f(4, length),
        hid=b(length, FF), dhid=b(length, FF),
        dmid=f(length, D), acc=f(10, 8, FF),
        gdown=f(FF, D), gup=f(D, FF), gout=f(D, D), gq=f(PAIRS, D, D),
        rows2=f(32, 128 + 6 * D), brow=f(1, 6 * D + sum(bias_lengths()[:4])),
        bg=f(groups, 1, sum(plan.biases)),
        cg_s=f(groups, 1, 128), cg_r=f(groups, 1, 128), nrm=f(groups, 1, 128),
        ls=dma(16), ws=dma(6, 3), wr=dma(6, 3), ts=dma(5, 3), tr=dma(5, 3),
        es=dma(n, 2 * layers), cs=dma(n, 7), cr=dma(n, 7), xs=dma(3, 5), xr=dma(3, 5), os=dma(16), st=dma(5, 3),
    )
    for i, width in enumerate(plan.widths):
        items[f"row{i}"] = f(groups, plan.reps, 1, width)
    kinds = {BF16: b, F32: f}
    for k, one in enumerate(plan.chunks):
        items[f"ra{k}"] = f(2, one.rows, one.cols)
        items[f"sb{k}"] = b(one.rows, one.cols)
        items[f"rb{k}"] = b(one.rows, one.cols)
        if not one.direct:
            items[f"sc{k}"] = kinds[HALF_TYPE](one.half, one.cols)
            items[f"rc{k}"] = kinds[HALF_TYPE](one.half, one.cols)
        halves = 2 if one.direct else 1
        items[f"hf{k}"] = f(halves * one.slabs, plan.unit, 128)
        if LAYER_TYPE is not F32:
            items[f"sd{k}"] = b(halves * one.slabs, plan.unit, 128)
        items[f"rd{k}"] = kinds[LAYER_TYPE](halves * layers, one.per, plan.unit, 128)
        items[f"ag{k}"] = kinds[SPREAD_TYPE](2, one.slabs, plan.unit, 128)
    return items


HALF_TYPE, LAYER_TYPE, SPREAD_TYPE = BF16, BF16, BF16


def encode(value):
    return (value * jnp.abs(value)).astype(BF16)


def decode(code):
    wide = code.astype(F32)
    return wide * lax.rsqrt(jnp.maximum(jnp.abs(wide), 1e-37))


class Refs:
    def __init__(self, names, refs):
        for name, ref in zip(names, refs, strict=True):
            setattr(self, name, ref)


ARGS = ["lat_h", "og_h", "cond", "mst_h", "one_h", "two_h", "bm_h"]
OUTS = ["out_h", "latg_h", "gpk_h", "none_h", "ntwo_h", "back", "squares", "bgrad"]


def at(value, step):
    return pl.multiple_of(value, step)


def step_kernel(plan, names, *refs):
    v = Refs(ARGS + OUTS + names, refs)
    groups, reps, layers, length = plan.groups, plan.reps, plan.layers, plan.length
    r, g = lax.axis_index("rep"), lax.axis_index("grp")
    h, zi, c, x = r % 2, r // 2, g % 2, g // 2
    g1, g2, g3, r1 = g + 1 - 2 * c, g + 2 - 4 * x, 3 - g, r + 1 - 2 * h
    others = [g1, g2, g3]
    part = D // groups

    def rdma(src, dst, send, recv, rep, grp):
        return pltpu.make_async_remote_copy(
            src_ref=src, dst_ref=dst, send_sem=send, recv_sem=recv,
            device_id=(rep, grp), device_id_type=pl.DeviceIdType.MESH,
        )

    def layer_rep(dz):
        return ((zi + dz) % layers) * 2 + h

    barrier = pltpu.get_barrier_semaphore()

    def greet(rep, grp):
        pl.semaphore_signal(barrier, inc=1, device_id=(rep, grp), device_id_type=pl.DeviceIdType.MESH)

    for t in others:
        greet(r, t)

    def any_rep(d):
        return ((zi + d // 2) % layers) * 2 + (h + d) % 2

    def greet_rep(d, _):
        greet(any_rep(d), g)
        return 0

    lax.fori_loop(1, reps, greet_rep, 0)

    def region_copy(src, dst, k, sem):
        base, count, _, _ = plan.regions[k]
        return pltpu.make_async_copy(src.at[pl.ds(base, count), :], dst.at[pl.ds(base, count), :], sem)

    loads = [region_copy(v.mst_h, v.mst, k, v.ls.at[k]) for k in range(5)]
    for k in (0, 4):
        loads[k].start()
    lat_in = pltpu.make_async_copy(v.lat_h, v.lat, v.ls.at[5])
    og_in = pltpu.make_async_copy(v.og_h, v.og, v.ls.at[6])
    one_in = pltpu.make_async_copy(v.one_h, v.one, v.ls.at[7])
    two_in = pltpu.make_async_copy(v.two_h, v.two, v.ls.at[8])
    lat_in.start()
    for k in (1, 2, 3):
        loads[k].start()

    cond = v.cond[...]
    sig = 1.0 / (1.0 + jnp.exp(-cond))
    act = (cond * sig).astype(BF16).astype(F32)
    v.act_s[...] = jnp.zeros_like(v.act_s)
    for j in range(groups):
        v.act_s[j, :, 0:part] = act[:, part * j : part * j + part]
    v.b_all[g] = v.bm_h[...].reshape(1, sum(plan.biases)).astype(BF16).astype(F32)

    def own(k, dst, first, place=lambda t: t):
        base, _, tiles, rows = plan.regions[k]
        for i in range(rows // part):
            for t in range(tiles):
                piece = v.mst[pl.ds(base + part * i * tiles + t, part, stride=tiles), :]
                dst[pl.ds(at(first + part * i, 32), part), 128 * place(t) : 128 * place(t) + 128] = piece.astype(BF16)

    mats = [v.w_qkv] * PAIRS + [v.w_out, v.w_up, v.w_down]
    kinds = [0] * PAIRS + [1, 2, 3]

    def pair_place(t):
        return (t % PAIRS) * 3 + t // PAIRS

    def weight_copy(k, route):
        rows = plan.regions[kinds[k]][3]
        block, to = [(g, g1), (g, g2), (g2, g1)][route]
        where = pl.ds(at(block * rows, 32), rows)
        ref = mats[k].at[where, D * k : D * k + D] if k < PAIRS else mats[k].at[where, :]
        return rdma(ref, ref, v.ws.at[k, route], v.wr.at[k, route], r, to)

    loads[0].wait()
    own(0, v.w_qkv, g * part, pair_place)
    pl.semaphore_wait(barrier, 3 + reps - 1)

    def to_others(kind, src, dst):
        return [
            rdma(src(t), dst, v.ts.at[kind, i], v.tr.at[kind, i], r, t) for i, t in enumerate(others)
        ]

    act_out = to_others(0, lambda t: v.act_s.at[t], v.act_r.at[g])
    bias_out = to_others(1, lambda t: v.b_all.at[g], v.b_all.at[g])
    mod_out = to_others(2, lambda t: v.mp_s.at[t], v.mp_r.at[g])
    for copy in act_out + bias_out:
        copy.start()
    weight_copy(0, 1).start()
    weight_copy(0, 0).start()
    v.act_r[g] = v.act_s[g]
    loads[4].wait()
    own(4, v.w_ada, 0)
    for copy in act_out:
        copy.wait_recv()
    left = jnp.concatenate([v.act_r[j][:, 0:part] for j in range(groups)] + [jnp.zeros((8 - groups, part), F32)], axis=0)
    parts = dot(left.astype(BF16), v.w_ada[...])
    for j in range(groups):
        v.mp_s[j] = parts[j : j + 1, :]
    for copy in mod_out:
        copy.start()
    v.mp_r[g] = v.mp_s[g]
    for p in range(1, PAIRS):
        weight_copy(p, 1).start()
        weight_copy(p, 0).start()
    og_in.start()
    for k in (1, 2, 3):
        loads[k].wait()
        own(k, mats[PAIRS - 1 + k], g * plan.regions[k][3])
        weight_copy(PAIRS - 1 + k, 1).start()
        weight_copy(PAIRS - 1 + k, 0).start()
        if k == 2:
            weight_copy(0, 1).wait_recv()
            weight_copy(0, 2).start()
    lat_in.wait()
    tile = 256
    tiles = length // tile

    def centre_tile(t, _):
        rows = pl.ds(at(t * tile, tile), tile)
        v.dmid[rows, :] = normalise(v.lat[rows, :].astype(F32))[0]
        return 0

    lax.fori_loop(0, tiles, centre_tile, 0)
    one_in.start()
    two_in.start()
    for copy in bias_out:
        copy.wait_recv()
    starts = [sum(plan.biases[:k]) for k in range(5)]

    def bias_row(k):
        s, n = starts[k], plan.biases[k]
        return jnp.concatenate([v.b_all[j][:, s : s + n] for j in range(groups)], axis=1)

    for k, ref in enumerate([v.b_qkv, v.b_out, v.b_up, v.b_down]):
        ref[...] = bias_row(k)
    flat = v.b_qkv[...]
    tiles_of = [flat[:, 128 * t : 128 * t + 128] for t in range(3 * PAIRS)]
    for t in range(3 * PAIRS):
        v.b_qkv[:, 128 * pair_place(t) : 128 * pair_place(t) + 128] = tiles_of[t]
    for copy in mod_out:
        copy.wait_recv()
    total = v.mp_r[0]
    for j in range(1, groups):
        total = total + v.mp_r[j]
    v.mod[...] = total + bias_row(4)

    def forward(k):
        weight_copy(k, 1).wait_recv()
        weight_copy(k, 2).start()

    def arrived(k):
        weight_copy(k, 0).wait_recv()
        weight_copy(k, 2).wait_recv()


    mod = v.mod
    shift1, scale1, gate1 = mod[:, 0:D], mod[:, D : 2 * D] + 1.0, mod[:, 2 * D : 3 * D]
    shift2, scale2, gate2 = mod[:, 3 * D : 4 * D], mod[:, 4 * D : 5 * D] + 1.0, mod[:, 5 * D : 6 * D]
    def norm_tile(t, _):
        rows = pl.ds(at(t * tile, tile), tile)
        v.nm1[rows, :] = (v.dmid[rows, :] * scale1 + shift1).astype(BF16)
        return 0

    lax.fori_loop(0, tiles, norm_tile, 0)

    def pair_cols(p):
        return pl.ds(at(p * D, D), D)

    def qkv_tile(p, t):
        rows = pl.ds(at(t * tile, tile), tile)
        proj = (dot(v.nm1[rows, :], v.w_qkv[:, pair_cols(p)]) + v.b_qkv[:, pair_cols(p)]).astype(BF16)
        v.q3[p, rows, :] = proj[:, 0:128] * jnp.asarray(HDIM**-0.5, BF16)
        v.k3[p, rows, :] = proj[:, 128:256]
        v.v3[p, rows, :] = proj[:, 256:384]

    qb = 256
    q_steps = length // qb

    def att_step(p, i):
        rows = pl.ds(at(i * qb, qb), qb)
        q = v.q3[p, rows, :]
        outs, stats = [], []
        for j in range(2):
            qj = jnp.where(lanes_of(j, qb), q, jnp.zeros_like(q))
            s = dot(qj, v.k3[p], NT)
            m = jnp.max(s, axis=-1, keepdims=True)
            e = jnp.exp(s - m)
            l = jnp.sum(e, axis=-1, keepdims=True)
            outs.append(dot((e * (1.0 / l)).astype(BF16), v.v3[p]))
            stats.append(m + jnp.log(l))
        v.att[p, rows, :] = jnp.where(lanes_of(0, qb), outs[0], outs[1]).astype(BF16)
        lane = lax.broadcasted_iota(jnp.int32, (qb, 128), 1)
        v.lse[p, :, rows] = jnp.where(lane == 0, stats[0], stats[1]).T[0:8, :]

    forwards = {(0, 0): [2], (0, 2): [3], (1, 2): [4], (2, 1): [5]}

    def att_pair(p, _):
        for k in range(PAIRS):
            @pl.when(p == k)
            def _(k=k):
                arrived(k)

        def project(t, _):
            qkv_tile(p, t)
            return 0

        lax.fori_loop(0, tiles, project, 0)

        @pl.when(p == 0)
        def _():
            forward(1)

        def attend(i, _):
            att_step(p, i)
            for (pp, ii), ks in forwards.items():
                @pl.when((p == pp) & (i == ii))
                def _(ks=ks):
                    for k in ks:
                        forward(k)
            return 0

        lax.fori_loop(0, q_steps, attend, 0)
        return 0

    lax.fori_loop(0, PAIRS, att_pair, 0)
    og_in.wait()
    for k in (3, 4, 5):
        arrived(k)

    acc = v.acc
    acc[...] = jnp.zeros_like(acc)

    def whole(i):
        return pl.ds(at(i * length, length), length)

    def spare_put(which, t, value):
        for i in range(PAIRS):
            v.dpj[pl.ds(at((which * PAIRS + i) * length + t * tile, tile), tile), :] = value[:, 128 * i : 128 * i + 128]

    def spare(which):
        return jnp.concatenate([v.dpj[whole(which * PAIRS + i), :] for i in range(PAIRS)], axis=1)

    def mlp_tile(t, _):
        rows = pl.ds(at(t * tile, tile), tile)
        atv = jnp.concatenate([v.att[p, rows, :] for p in range(PAIRS)], axis=1)
        branch1 = dot(atv, v.w_out[...]) + v.b_out[...]
        mid = v.lat[rows, :].astype(F32) + gate1 * branch1
        n2, r2 = normalise(mid)
        normed = (n2 * scale2 + shift2).astype(BF16)
        spare_put(0, t, normed)
        pre = dot(normed, v.w_up[...]) + v.b_up[...]
        sq = pre * pre
        th = jnp.tanh(pre * (GELU_C + (GELU_C * GELU_A) * sq))
        half = 0.5 + 0.5 * th
        hd = (pre * half).astype(BF16)
        v.hid[rows, :] = hd
        slope = half + (0.5 * pre) * (1.0 - th * th) * (GELU_C + (3.0 * GELU_C * GELU_A) * sq)
        branch2 = dot(hd, v.w_down[...]) + v.b_down[...]
        og = v.og[rows, :].astype(F32)
        v.og[rows, :] = (mid + gate2 * branch2).astype(BF16)
        d2 = (gate2 * og).astype(BF16)
        spare_put(1, t, d2)
        dh = (dot(d2, v.w_down[...], NT) * slope).astype(BF16)
        v.dhid[rows, :] = dh
        dn2 = dot(dh, v.w_up[...], NT)
        dm = og + norm_back(dn2 * scale2, n2, r2)
        v.dmid[rows, :] = dm
        d1 = (gate1 * dm).astype(BF16)
        spare_put(2, t, d1)
        da = dot(d1, v.w_out[...], NT).astype(BF16)
        for p in range(PAIRS):
            v.datt[p, rows, :] = da[:, 128 * p : 128 * p + 128]
        acc[2, :, 0:D] += fold(dm * branch1)
        acc[3, :, 0:D] += fold(dn2)
        acc[4, :, 0:D] += fold(dn2 * n2)
        acc[5, :, 0:D] += fold(og * branch2)
        acc[6, :, 0:D] += fold(d1.astype(F32))
        acc[7, :, 0:D] += fold(d2.astype(F32))
        acc[8, :, :] += fold(dh.astype(F32))
        return 0

    lax.fori_loop(0, tiles, mlp_tile, 0)
    out_copy = pltpu.make_async_copy(v.og, v.out_h, v.os.at[0])
    out_copy.start()

    def total_of(i, width):
        return jnp.sum(acc[i], axis=0, keepdims=True)[:, 0:width]

    def low_row(i):
        return total_of(i, D).astype(BF16).astype(F32)

    rowbufs = [v.row0, v.row1, v.row2]

    def row_put(n, pieces):
        ref, place = rowbufs[n].at[g, r], 0
        for piece in pieces:
            ref[:, place : place + piece.shape[1]] = piece
            place += piece.shape[1]

    def row_spread(n, d):
        ref = rowbufs[n].at[g, r]
        return rdma(ref, ref, v.xs.at[n, 0], v.xr.at[n, 0], any_rep(d), g)

    def row_wait(n, sems):
        few = rowbufs[n].at[g, pl.ds(0, reps - 1)]
        return pltpu.make_async_copy(few, few, sems.at[n, 0])

    def row_copies(n):
        ref = rowbufs[n]
        last = (ref.at[g], g3) if n == 2 else (ref.at[g2], g1)
        pairs = [(ref.at[g], g1), (ref.at[g], g2), last]
        return [rdma(src, src, v.xs.at[n, 1 + i], v.xr.at[n, 1 + i], r, to) for i, (src, to) in enumerate(pairs)]

    def row_step(n, stage):
        copies = row_copies(n)
        if stage == 0:
            def send_row(d, _):
                row_spread(n, d).start()
                return 0

            lax.fori_loop(1, reps, send_row, 0)
        elif stage == 1:
            row_wait(n, v.xr).wait()
            copies[1].start()
            copies[0].start()
            if n == 2:
                copies[2].start()
        elif stage == 2 and n < 2:
            copies[1].wait_recv()
            copies[2].start()
        else:
            for copy in copies if n == 2 else [copies[0], copies[2]]:
                copy.wait_recv()

    def row_sent(n):
        row_wait(n, v.xs).wait()
        for copy in row_copies(n):
            copy.wait_send()

    row_put(0, [v.act_s[j] for j in range(groups)] + [low_row(i) for i in range(2, 6)]
            + [total_of(6, D), total_of(8, FF), total_of(7, D)])
    row_step(0, 0)

    def grad_of(k):
        one = plan.chunks[k]
        return v.gq.at[one.pair] if one.pair is not None else getattr(v, one.name)

    def buf(k, *names):
        return [getattr(v, f"{name}{k}") for name in names]

    def copy_a(k, kk):
        one = plan.chunks[k]
        (ra,) = buf(k, "ra")
        rows = pl.ds(at((2 * kk + 1 - c) * one.stride + one.row0, 32), one.rows)
        src = grad_of(k).at[rows, one.col0 : one.col0 + one.cols]
        return rdma(src, ra.at[kk], v.cs.at[k, 5 + kk], v.cr.at[k, 5 + kk], r, g1)

    def copy_b(k):
        sb, rb = buf(k, "sb", "rb")
        return rdma(sb, rb, v.cs.at[k, 0], v.cr.at[k, 0], r, g2)

    def copy_c(k):
        sc, rc = buf(k, "sc", "rc")
        return rdma(sc, rc, v.cs.at[k, 1], v.cr.at[k, 1], r1, g)

    def copy_f(k):
        (ag,) = buf(k, "ag")
        return rdma(ag.at[h], ag.at[h], v.cs.at[k, 4], v.cr.at[k, 4], r1, g)

    def by_rows(rows, body):
        def run(i, _):
            body(at(i * plan.unit, 16))
            return 0

        lax.fori_loop(0, rows // plan.unit, run, 0)

    def rows_at(value):
        return pl.ds(at(value, 16), plan.unit)

    def s1(k):
        for kk in range(2):
            copy_a(k, kk).start()

    def s2(k):
        one = plan.chunks[k]
        ra, sb = buf(k, "ra", "sb")
        for kk in range(2):
            copy_a(k, kk).wait_recv()
        first = (2 * (1 - x) + c) * one.stride + one.row0
        cols = slice(one.col0, one.col0 + one.cols)

        def body(i):
            sb[rows_at(i), :] = encode(grad_of(k)[rows_at(first + i), cols] + ra[1 - x, rows_at(i), :])

        by_rows(one.rows, body)
        copy_b(k).start()

    def s3(k):
        one = plan.chunks[k]
        ra, rb, sc = buf(k, "ra", "rb", "sc")
        copy_b(k).wait_recv()
        first = (1 - h) * one.half
        cols = slice(one.col0, one.col0 + one.cols)

        def body(i):
            mine = grad_of(k)[rows_at(g * one.stride + one.row0 + first + i), cols]
            total = mine + ra[x, rows_at(first + i), :] + decode(rb[rows_at(first + i), :])
            sc[rows_at(i), :] = encode(total)

        by_rows(one.half, body)
        copy_c(k).start()

    def set_at(k, q):
        return pl.ds(q * plan.chunks[k].per, plan.chunks[k].per)

    def sent_slabs(k):
        return buf(k, "hf")[0] if LAYER_TYPE is F32 else buf(k, "sd")[0]

    def copy_d(k, q, to):
        (rd,) = buf(k, "rd")
        slot = (zi - to + layers) % layers
        return rdma(sent_slabs(k).at[set_at(k, q)], rd.at[slot], v.cs.at[k, 2], v.cr.at[k, 2], to * 2 + h, g)

    def s4(k):
        one = plan.chunks[k]
        ra, rb, rc, hf = buf(k, "ra", "rb", "rc", "hf")
        copy_c(k).wait_recv()
        first = h * one.half
        for s in range(one.slabs):
            i, col = one.slab(s)
            cols = slice(col, col + 128)
            near = pl.ds(at(first + i, 16), plan.unit)
            mine = grad_of(k)[rows_at(g * one.stride + one.row0 + first + i), one.col0 + col : one.col0 + col + 128]
            far = decode(rb[near, cols]) + decode(rc[i : i + plan.unit, cols])
            value = mine + ra[x, near, cols] + far
            hf[s] = value
            if LAYER_TYPE is not F32:
                buf(k, "sd")[0][s] = encode(value)
        for q in range(one.sets):
            to = (q + k) % layers

            @pl.when(to != zi)
            def _(q=q, to=to):
                copy_d(k, q, to).start()

    def mine_of(k):
        return (zi - k % layers + layers) % layers

    def slab_bytes(k, count, sem, name):
        if name == "ag":
            ref = buf(k, "ag")[0].at[0, pl.ds(0, count * plan.chunks[k].per)]
        else:
            ref = buf(k, "rd")[0].at[pl.ds(0, count)]
        return pltpu.make_async_copy(ref, ref, sem)

    def copy_e(k, q, dz):
        (ag,) = buf(k, "ag")
        ref = ag.at[h, set_at(k, q)]
        return rdma(ref, ref, v.es.at[k, dz], v.cr.at[k, 3], layer_rep(dz), g)

    def s5(k):
        one = plan.chunks[k]
        hf, rd, ag = buf(k, "hf", "rd", "ag")
        q, per = mine_of(k), one.per

        @pl.when(q < one.sets)
        def _():
            slab_bytes(k, layers - 1, v.cr.at[k, 2], "rd").wait()
            for i in range(per):
                def add(z, value):
                    return value + decode(rd[z, i])

                value = lax.fori_loop(1, layers, add, hf[q * per + i], unroll=layers <= 4)
                ag[h, q * per + i] = encode(value)

            def send(dz, _):
                copy_e(k, q, dz).start()
                return 0

            lax.fori_loop(1, layers, send, 0)

    def s6(k):
        sets = plan.chunks[k].sets

        @pl.when(mine_of(k) < sets)
        def _():
            slab_bytes(k, sets - 1, v.cr.at[k, 3], "ag").wait()

        @pl.when(mine_of(k) >= sets)
        def _():
            slab_bytes(k, sets, v.cr.at[k, 3], "ag").wait()

        copy_f(k).start()

    def s7(k):
        copy_f(k).wait_recv()
        unpack(k)

    def unpack(k):
        one = plan.chunks[k]
        (ag,) = buf(k, "ag")
        base, _, across, _ = plan.regions[one.kind]
        for half in range(2):
            for s in range(one.slabs):
                first = base + (one.row0 + half * one.half + one.slab(s)[0]) * across + one.tile(s)
                v.gpk[pl.ds(first, plan.unit, stride=across), :] = decode(ag[half, s])

    def sent(k):
        sets = plan.chunks[k].sets
        for kk in range(0 if k in (2, 3) else 2):
            copy_a(k, kk).wait_send()
        copy_b(k).wait_send()
        copy_c(k).wait_send()
        copy_f(k).wait_send()

        @pl.when(mine_of(k) < sets)
        def _():
            slab_bytes(k, sets - 1, v.cs.at[k, 2], "rd").wait()
            spread(k, layers - 1)

        @pl.when(mine_of(k) >= sets)
        def _():
            slab_bytes(k, sets, v.cs.at[k, 2], "rd").wait()

    def spread(k, count):
        def wait(dz, _):
            copy_e(k, mine_of(k), dz).wait_send()
            return 0

        lax.fori_loop(1, 1 + count, wait, 0)

    def direct_out(k, hh, q):
        sd, rd = buf(k, "sd", "rd")
        to = (q + k) % layers
        slot = ((zi - to + layers) % layers) * 2 + (h - hh) % 2
        src = sd.at[pl.ds((hh * plan.chunks[k].sets + q) * plan.chunks[k].per, plan.chunks[k].per)]
        return rdma(src, rd.at[slot], v.cs.at[k, 2], v.cr.at[k, 2], to * 2 + hh, g)

    def direct_back(k, d):
        (ag,) = buf(k, "ag")
        ref = ag.at[h, set_at(k, mine_of(k))]
        return rdma(ref, ref, v.es.at[k, d], v.cr.at[k, 3], any_rep(d), g)

    def d3(k):
        one = plan.chunks[k]
        ra, rb, hf, sd = buf(k, "ra", "rb", "hf", "sd")
        copy_b(k).wait_recv()
        for hh in range(2):
            for s in range(one.slabs):
                i, col = one.slab(s)
                i = i + hh * one.half
                cols = slice(col, col + 128)
                mine = grad_of(k)[rows_at(g * one.stride + one.row0 + i), one.col0 + col : one.col0 + col + 128]
                value = mine + ra[x, i : i + plan.unit, cols] + decode(rb[i : i + plan.unit, cols])
                hf[hh * one.slabs + s] = value
                sd[hh * one.slabs + s] = encode(value)
        for hh in range(2):
            for q in range(one.sets):
                @pl.when(((q + k) % layers != zi) | (hh != h))
                def _(hh=hh, q=q):
                    direct_out(k, hh, q).start()

    def d5(k):
        one = plan.chunks[k]
        hf, rd, ag = buf(k, "hf", "rd", "ag")
        q, per = mine_of(k), one.per

        @pl.when(q < one.sets)
        def _():
            slab_bytes(k, reps - 1, v.cr.at[k, 2], "rd").wait()
            for i in range(per):
                def add(d, value):
                    return value + decode(rd[d, i])

                value = lax.fori_loop(1, reps, add, hf[h * one.slabs + q * per + i], unroll=reps <= 8)
                ag[h, q * per + i] = encode(value)

            def send(d, _):
                direct_back(k, d).start()
                return 0

            lax.fori_loop(1, reps, send, 0)

    def d7(k):
        sets = plan.chunks[k].sets

        @pl.when(mine_of(k) < sets)
        def _():
            slab_bytes(k, 2 * sets - 1, v.cr.at[k, 3], "rd").wait()

        @pl.when(mine_of(k) >= sets)
        def _():
            slab_bytes(k, 2 * sets, v.cr.at[k, 3], "rd").wait()

        unpack(k)

    def direct_sent(k):
        sets = plan.chunks[k].sets
        for kk in range(2):
            copy_a(k, kk).wait_send()
        copy_b(k).wait_send()

        @pl.when(mine_of(k) < sets)
        def _():
            slab_bytes(k, 2 * sets - 1, v.cs.at[k, 2], "rd").wait()

            def wait(d, _):
                direct_back(k, d).wait_send()
                return 0

            lax.fori_loop(1, reps, wait, 0)

        @pl.when(mine_of(k) >= sets)
        def _():
            slab_bytes(k, 2 * sets, v.cs.at[k, 2], "rd").wait()

    direct_steps = {"1": s1, "2": s2, "3": d3, "5": d5, "7": d7}
    steps = dict(zip("1234567", (s1, s2, s3, s4, s5, s6, s7)))

    def run(text):
        for word in text:
            if word[0] == "r":
                row_step(int(word[1]), int(word[2]))
            else:
                k = int(word[1])
                (direct_steps if plan.chunks[k].direct else steps)[word[0]](k)

    def stores(k):
        pairs = ((v.gpk, v.gpk_h), (v.one, v.none_h), (v.two, v.ntwo_h))
        return [region_copy(a, b, k, v.st.at[k, i]) for i, (a, b) in enumerate(pairs)]

    def whole_sum(one):
        return jnp.sum(jnp.sum(one, axis=1, keepdims=True), axis=0, keepdims=True)

    def lamb(k):
        base, count, _, _ = plan.regions[k]

        size = 288

        def body(i, sums):
            rows = pl.ds(at(base + i * size, 32), size)
            grad, w = v.gpk[rows, :], v.mst[rows, :]
            move, v.one[rows, :], v.two[rows, :] = adam(v.one[rows, :], v.two[rows, :], grad)
            update = move + DECAY_RATE * w
            v.gpk[rows, :] = update
            return sums[0] + fold(w * w), sums[1] + fold(update * update)

        zero = jnp.zeros((8, 128), F32)
        sums = lax.fori_loop(0, count // size, body, (zero, zero))
        for copy in stores(k):
            copy.start()
        return [whole_sum(one) for one in sums]

    def g_down(i, _):
        cols = pl.ds(at(i * D, D), D)
        v.gdown[cols, :] = dot(v.hid[:, cols], spare(1), TN)
        return 0

    def g_up(i, _):
        cols = pl.ds(at(i * D, D), D)
        v.gup[:, cols] = dot(spare(0), v.dhid[:, cols], TN)
        return 0

    lax.fori_loop(0, FF // D, g_down, 0)
    run(["10", "11"])
    lax.fori_loop(0, FF // D // 2, g_up, 0)
    run(["20", "12"])
    lax.fori_loop(FF // D // 2, FF // D, g_up, 0)
    run(["21", "13"])
    for p in range(PAIRS):
        v.gout[128 * p : 128 * p + 128, :] = dot(v.att[p], spare(2), TN)
    run(["22", "14"])

    kb = 256
    k_steps = length // kb
    after = {
        0: ["23", "24"], 2: ["30"], 3: ["15", "31"], 4: ["25", "32", "40"], 5: ["33", "r01"],
        6: ["34", "41", "42"], 7: ["16", "35", "43", "50"], 8: ["26", "44", "51"],
        9: ["52", "55", "r02"], 10: ["53", "60"], 11: ["17", "36", "61", "62", "54"],
    }

    def att_back(it, _):
        p, b = it // k_steps, it % k_steps
        do, q = v.datt[p], v.q3[p]

        @pl.when(b == 0)
        def _():
            prod = (do.astype(F32) * v.att[p].astype(F32)).T
            v.stt[0:2, :] = v.lse[p, 0:2, :]
            for j in range(2):
                v.stt[2 + j : 3 + j, :] = jnp.sum(prod[HDIM * j : HDIM * j + HDIM, :], axis=0, keepdims=True)
            v.dqs[...] = jnp.zeros_like(v.dqs)

        rows = pl.ds(at(b * kb, kb), kb)
        kk, vv = v.k3[p, rows, :], v.v3[p, rows, :]
        dv, dk, dq = [], [], []
        for j in range(2):
            keep = lanes_of(j, length)
            dos = jnp.where(keep, do, jnp.zeros_like(do))
            qs = jnp.where(keep, q, jnp.zeros_like(q))
            pt = jnp.exp(dot(kk, qs, NT) - v.stt[j : j + 1, :])
            dst = (pt * (dot(vv, dos, NT) - v.stt[2 + j : 3 + j, :])).astype(BF16)
            dv.append(dot(pt.astype(BF16), dos))
            dk.append(dot(dst, qs))
            kj = jnp.where(lanes_of(j, kb), kk, jnp.zeros_like(kk))
            dq.append(dot(dst, kj, TN))
        v.dpj[pl.ds(at((2 * PAIRS + p) * length + b * kb, kb), kb), :] = (dv[0] + dv[1]).astype(BF16)
        v.dpj[pl.ds(at((PAIRS + p) * length + b * kb, kb), kb), :] = (dk[0] + dk[1]).astype(BF16)
        v.dqs[...] += dq[0] + dq[1]

        @pl.when(b == k_steps - 1)
        def _():
            v.dpj[whole(p), :] = (v.dqs[...] * (HDIM**-0.5)).astype(BF16)
            cols = jnp.concatenate([v.dpj[whole(i * PAIRS + p), :] for i in range(3)], axis=1)
            v.gq[p] = dot(v.nm1[...], cols, TN)
            acc[9, :, pair_cols(p)] = fold(cols.astype(F32))

        for i, text in after.items():
            @pl.when(it == i)
            def _(text=text):
                run(text)
        return 0

    lax.fori_loop(0, PAIRS * k_steps, att_back, 0)

    row_put(1, [total_of(9, 3 * D)])
    row_step(1, 0)

    for k in (2, 3):
        for kk in range(2):
            copy_a(k, kk).wait_send()

    def last_tile(t, _):
        rows = pl.ds(at(t * tile, tile), tile)
        order = [k * PAIRS + p for p in range(PAIRS) for k in range(3)]
        dp = jnp.concatenate([v.dpj[pl.ds(at(i * length + t * tile, tile), tile), :] for i in order], axis=1)
        dn1 = dot(dp, v.w_qkv[...], NT)
        n1, _r = normalise(v.lat[rows, :].astype(F32))
        v.gup[0:tile, pair_cols(t)] = dn1
        acc[0, :, 0:D] += fold(dn1)
        acc[1, :, 0:D] += fold(dn1 * n1)
        for i, text in {0: ["27", "70", "r03"], 1: ["r11", "63"], 2: ["75"], 3: ["71", "72", "64", "56"]}.items():
            @pl.when(t == i)
            def _(text=text):
                run(text)
        return 0

    lax.fori_loop(0, tiles, last_tile, 0)
    row_put(2, [low_row(0), low_row(1)])
    run(["r20", "37"])

    def latent_tile(t, _):
        rows = pl.ds(at(t * tile, tile), tile)
        n1, rs1 = normalise(v.lat[rows, :].astype(F32))
        v.lat[rows, :] = (v.dmid[rows, :] + norm_back(v.gup[0:tile, pair_cols(t)] * scale1, n1, rs1)).astype(BF16)
        return 0

    lax.fori_loop(0, tiles, latent_tile, 0)
    latg_copy = pltpu.make_async_copy(v.lat, v.latg_h, v.os.at[11])
    latg_copy.start()

    one_in.wait()
    two_in.wait()
    sums = [None] * 5
    sums[3] = lamb(3)
    run(["r21", "73"])
    sums[2] = lamb(2)
    m0 = 128 * groups
    base, _, across, _ = plan.regions[4]
    v.brow[...] = jnp.zeros_like(v.brow)
    v.gpk[base : base + part * across, :] = jnp.zeros((part * across, 128), F32)

    def ada(late):
        tiles_of = range(0, 2 * D // 128) if late else range(2 * D // 128, across)

        def rows_of(n, _):
            one_sum, two_sum = [], []
            for i in range(32):
                j = n * 32 + i
                early, mid, end = [ref.at[j // reps, j % reps] for ref in rowbufs]
                v.rows2[i : i + 1, 0:128] = early[:, pl.ds(at(g * 128, 128), 128)]
                if late:
                    v.rows2[i : i + 1, 128 : 128 + 2 * D] = end[...]
                    one_sum.append(end[...])
                    two_sum.append(mid[...])
                else:
                    v.rows2[i : i + 1, 128 + 2 * D :] = early[:, m0 : m0 + 4 * D]
                    one_sum.append(early[:, m0 : m0 + 4 * D])
                    two_sum.append(early[:, m0 + 4 * D :])
            spans = ((0, 2 * D), (6 * D, 9 * D)) if late else ((2 * D, 6 * D), (9 * D, v.brow.shape[1]))
            for (low, high), pieces in zip(spans, (one_sum, two_sum)):
                v.brow[:, low:high] += sum(pieces[1:], pieces[0])
            acts = v.rows2[:, 0:128].astype(BF16)
            for t in tiles_of:
                piece = dot(acts, v.rows2[:, 128 * t + 128 : 128 * t + 256].astype(BF16), TN)[0:part, :]
                rows = pl.ds(base + t, part, stride=across)
                v.gpk[rows, :] = v.gpk[rows, :] + piece
            return 0

        lax.fori_loop(0, reps * groups // 32, rows_of, 0)
        total = [jnp.zeros((8, 128), F32)] * 2
        for t in tiles_of:
            rows = pl.ds(base + t, part, stride=across)
            w = v.mst[rows, :]
            move, first, second = adam(v.one[rows, :], v.two[rows, :], v.gpk[rows, :])
            update = move + DECAY_RATE * w
            v.one[rows, :] = first
            v.two[rows, :] = second
            v.gpk[rows, :] = update
            total = [total[0] + fold(w * w), total[1] + fold(update * update)]
        return total

    run(["57", "r12", "74"])
    early_sums = ada(False)
    sums[1] = lamb(1)
    run(["76", "r13", "r22"])
    late_sums = ada(True)

    dm4 = jnp.concatenate(
        [
            jnp.concatenate([v.row2[j, r], v.row0[j, r][:, m0 : m0 + 4 * D]], axis=1) for j in range(groups)
        ] + [jnp.zeros((8 - groups, 6 * D), F32)], axis=0
    )
    dact = dot(dm4.astype(BF16), v.w_ada[...], NT)
    v.cg_s[...] = jnp.zeros_like(v.cg_s)
    for j in range(groups):
        v.cg_s[j, :, 0:part] = dact[j : j + 1, :]
    cg_out = to_others(3, lambda t: v.cg_s.at[t], v.cg_r.at[g])
    for copy in cg_out:
        copy.start()
    v.cg_r[g] = v.cg_s[g]

    for copy in stores(4):
        copy.start()
    sums[4] = [whole_sum(a + b) for a, b in zip(early_sums, late_sums)]
    run(["77"])
    sums[0] = lamb(0)
    lane = lax.broadcasted_iota(jnp.int32, (1, 128), 1)
    packed = jnp.zeros((1, 128), F32)
    for k in range(5):
        packed = jnp.where(lane == k, sums[k][0], packed)
        packed = jnp.where(lane == 8 + k, sums[k][1], packed)
    v.nrm[g] = packed
    nrm_out = to_others(4, lambda t: v.nrm.at[g], v.nrm.at[g])
    for copy in nrm_out:
        copy.start()

    sumrow = v.brow[...]
    flat = sumrow[:, 6 * D : 9 * D]
    qkv_row = jnp.concatenate(
        [flat[:, 128 * pair_place(t) : 128 * pair_place(t) + 128] for t in range(3 * PAIRS)], axis=1
    )
    rest = sumrow[:, 9 * D :]
    grads_of = [qkv_row, rest[:, 0:D], rest[:, D : D + FF], rest[:, D + FF :], sumrow[:, 0 : 6 * D]]
    for j in range(groups):
        v.bg[j] = jnp.concatenate([one[:, n * j : n * j + n] for one, n in zip(grads_of, plan.biases)], axis=1)
    v.bgrad[...] = v.bg[g]

    for copy in cg_out:
        copy.wait_recv()
    back = jnp.concatenate([v.cg_r[j][:, 0:part] for j in range(groups)], axis=1)
    v.back[...] = back

    for copy in nrm_out:
        copy.wait_recv()
    squares = v.nrm[0]
    for j in range(1, groups):
        squares = squares + v.nrm[j]
    v.squares[...] = squares

    for k in range(6):
        for route in range(3):
            weight_copy(k, route).wait_send()
    for copy in act_out + bias_out + mod_out + cg_out + nrm_out:
        copy.wait_send()
    for k, one in enumerate(plan.chunks):
        (direct_sent if one.direct else sent)(k)
    for n in range(3):
        row_sent(n)
    out_copy.wait()
    latg_copy.wait()
    for k in range(5):
        for copy in stores(k):
            copy.wait()


def finish_kernel(plan, refs_in, refs_out, scratch):
    out_i, latg_i, upd, one, two, back, squares, bgrad, cond, mst, bm, b1, b2 = refs_in
    out_o, latg_o, condg, stats, nmst, none, ntwo, ncpy, nb, nb1, nb2, nbc = refs_out
    upd_v, mst_v, one_v, two_v, cpy_v, out_v, latg_v, scales, sem_in, sem_out, sem_b = scratch
    size = plan.regions[0][1]
    blocks = plan.rows // size

    def part(i):
        return pl.ds(at(i * size, 32), size)

    def load(i):
        pairs = ((upd, upd_v), (mst, mst_v))
        return [pltpu.make_async_copy(a.at[part(i), :], b.at[part(i), :], sem_in.at[i, n]) for n, (a, b) in enumerate(pairs)]

    def store(i):
        pairs = ((mst_v, nmst), (cpy_v, ncpy))
        return [pltpu.make_async_copy(a.at[part(i), :], b.at[part(i), :], sem_out.at[i, n]) for n, (a, b) in enumerate(pairs)]

    moves = [(one, one_v, none), (two, two_v, ntwo), (out_i, out_v, out_o), (latg_i, latg_v, latg_o)]
    arrive = [pltpu.make_async_copy(a, b, sem_b.at[n]) for n, (a, b, _c) in enumerate(moves)]
    leave = [pltpu.make_async_copy(b, d, sem_b.at[4 + n]) for n, (_a, b, d) in enumerate(moves)]
    for copy in arrive[0:1]:
        copy.start()
    for i in range(blocks):
        for copy in load(i):
            copy.start()
    for copy in arrive[1:]:
        copy.start()

    norms = jnp.sqrt(squares[...])
    weight_norm, update_norm = norms[:, 0:5], norms[:, 8:13]
    ratio = weight_norm / (update_norm + NORM_EPS)
    stats[0:1, :] = weight_norm
    stats[1:2, :] = update_norm
    stats[2:3, :] = ratio
    for k in range(5):
        scales[k] = jnp.broadcast_to(ratio[:, k : k + 1], (8, 128))
    sig = 1.0 / (1.0 + jnp.exp(-cond[...]))
    condg[...] = back[...] * (sig * (1.0 + cond[...] * (1.0 - sig)))
    move, first, second = adam(b1[...], b2[...], bgrad[...].reshape(bm.shape))
    fresh = bm[...] - STEP_RATE * move
    nb[...] = fresh
    nb1[...] = first
    nb2[...] = second
    nbc[...] = fresh.astype(BF16)

    arrive[0].wait()
    leave[0].start()
    edges = [base for base, _, _, _ in plan.regions] + [plan.rows]
    for i in range(blocks):
        for copy in load(i):
            copy.wait()
        for k in range(5):
            low, high = max(edges[k], i * size), min(edges[k + 1], (i + 1) * size)
            if low < high:
                scale = jnp.broadcast_to(scales[k][0:1, :], (96, 128))

                def apply(n, _, low=low, scale=scale):
                    rows = pl.ds(at(low + n * 96, 32), 96)
                    value = mst_v[rows, :] - STEP_RATE * (scale * upd_v[rows, :])
                    mst_v[rows, :] = value
                    cpy_v[rows, :] = value.astype(BF16)
                    return 0

                lax.fori_loop(0, (high - low) // 96, apply, 0)
        for copy in store(i):
            copy.start()
    for n in (1, 2, 3):
        arrive[n].wait()
        leave[n].start()
    for copy in leave:
        copy.wait()
    for i in range(blocks):
        for copy in store(i):
            copy.wait()


def local(
    latents, condition, out_grad, master, moment_one, moment_two, bias_master, bias_one, bias_two
):
    groups, reps = lax.axis_size("grp"), lax.axis_size("rep")
    plan = Plan(groups, reps, latents.shape[0])
    items = scratch_of(plan)
    names = list(items)
    sds = jax.ShapeDtypeStruct
    full = lambda dtype: sds(master.shape, dtype)
    count = bias_master.shape[0]
    act = sds(latents.shape, BF16)
    hbm, vmem = pl.BlockSpec(memory_space=pl.ANY), pl.BlockSpec(memory_space=pltpu.VMEM)
    held = pl.pallas_call(
        lambda *refs: step_kernel(plan, names, *refs),
        out_shape=(act, act, full(F32), full(F32), full(F32), sds((1, D), F32), sds((1, 128), F32), sds((1, count), F32)),
        in_specs=[hbm, hbm, vmem, hbm, hbm, hbm, vmem],
        out_specs=[hbm] * 5 + [vmem] * 3,
        scratch_shapes=list(items.values()),
        compiler_params=pltpu.CompilerParams(
            vmem_limit_bytes=67043328, collective_id=0, has_side_effects=True
        ),
        name="step",
    )(latents, out_grad, condition, master, moment_one, moment_two, bias_master)
    blocks = plan.rows // plan.regions[0][1]
    line = lambda dtype: sds((count,), dtype)
    f = lambda *shape: pltpu.VMEM(shape, F32)
    return pl.pallas_call(
        lambda *refs: finish_kernel(plan, refs[:13], refs[13:25], refs[25:]),
        out_shape=(
            act, act, sds(condition.shape, F32), sds((3, 5), F32),
            full(F32), full(F32), full(F32), full(BF16), line(F32), line(F32), line(F32), line(BF16),
        ),
        in_specs=[hbm] * 5 + [vmem] * 4 + [hbm] + [vmem] * 3,
        out_specs=[hbm, hbm, vmem, vmem, hbm, hbm, hbm, hbm, vmem, vmem, vmem, vmem],
        scratch_shapes=[
            f(plan.rows, 128), f(plan.rows, 128), f(plan.rows, 128), f(plan.rows, 128),
            pltpu.VMEM((plan.rows, 128), BF16), pltpu.VMEM(latents.shape, BF16), pltpu.VMEM(latents.shape, BF16),
            f(5, 8, 128), pltpu.SemaphoreType.DMA((blocks, 2)), pltpu.SemaphoreType.DMA((blocks, 2)),
            pltpu.SemaphoreType.DMA((8,)),
        ],
        compiler_params=pltpu.CompilerParams(vmem_limit_bytes=67043328),
        name="finish",
    )(*held, condition, master, bias_master, bias_one, bias_two)


def solution(mesh):
    row, own, vec = P(("rep", "grp"), None), P("grp", None), P("grp")
    return jax.shard_map(
        local,
        mesh=mesh,
        in_specs=(row, row, row, own, own, own, vec, vec, vec),
        out_specs=(row, row, row, P(), own, own, own, own, vec, vec, vec, vec),
        check_vma=False,
    )
```
